32 devices in a mesh: gy: 4 (over x, core), gx: 8 (over z, y).
Axes of the slice: x: 2, y: 2, z: 4, core: 2. Of those that a mesh axis runs over, the one named last changes fastest.
Arguments:
- control: float32 [64, 512], P('gx', 'gy'), may hold values from -6 to 6
- background_std: float32 [64, 512], P('gx', 'gy'), may hold values from 0.1 to 1.9
- class_index: int32 [2, 64, 512], P(None, 'gx', 'gy'), may hold values from 0 to 23
- rate_table: float32 [2, 24], replicated
- brightness: float32 [2, 128], P(None, 'gx'), may hold values from 0 to 0.9
- circumsolar: float32 [128, 256], P('gx'), may hold values from 0 to 3
- isotropic: float32 [256], replicated, may hold values from 0.5 to 1
- horizon: float32 [256], replicated, may hold values from 0 to 1
- obs_cell: int32 [8, 4, 1024], P('gx', 'gy'), may hold values from 0 to 1023
- obs_subhour: int32 [8, 4, 1024], P('gx', 'gy'), may hold values from 0 to 127
- obs_orient: int32 [8, 4, 1024], P('gx', 'gy'), may hold values from 0 to 255
- obs_value: float32 [8, 4, 1024], P('gx', 'gy'), may hold values from -6 to 6
Outputs:
- increment: float32 [64, 512], P('gx', 'gy')
- departure: float32 [8, 4, 1024], P('gx', 'gy')
The draws below stay inside these ranges and needn't reach their ends.
All inputs are finite; a program needn't handle non-finite values.
Results may differ from the reference program's by a relative error of at most 0.00002.
Values sent between devices are 32-bit elements; how exact they have to be, the bound alone decides.
No kernel may reach another device: no remote copies, remote signals or barrier semaphores. Data moves between devices by JAX's collectives and lax.ppermute only.
A program may use at most 64 MiB of HBM per device.

```python
import jax
import jax.numpy as jnp
from jax import lax

CX = 8
CY = 128
SCALE_CLASSES = 24
ORIENT = 256
OBS_DEV = 1024
CELLS_ALONG_X = 64
CELLS_ALONG_Y = 512
SUBHOURS = 128
N_GY = 4
N_GX = 8


def draw_class_index(key, part):
    random_child_keys = jax.random.split(key, 10)
    third_random_key = SCALE_CLASSES // 3
    rough_x = jax.random.randint(random_child_keys[0], (1, CELLS_ALONG_Y), 0, 2)
    baseline_rate_x = jnp.where(rough_x == 1, jax.random.randint(random_child_keys[1], (CELLS_ALONG_X, CELLS_ALONG_Y), third_random_key, 2 * third_random_key), jax.random.randint(random_child_keys[2], (CELLS_ALONG_X, CELLS_ALONG_Y), 0, third_random_key))
    sudden_rate_x = jax.random.randint(random_child_keys[3], (CELLS_ALONG_X, CELLS_ALONG_Y), 0, CELLS_ALONG_X) < 2
    length_class_x = jnp.where(sudden_rate_x, jax.random.randint(random_child_keys[4], (CELLS_ALONG_X, CELLS_ALONG_Y), 2 * third_random_key, SCALE_CLASSES), baseline_rate_x)
    rough_y = jax.random.randint(random_child_keys[5], (CELLS_ALONG_X, 1), 0, 2)
    baseline_rate_y = jnp.where(rough_y == 1, jax.random.randint(random_child_keys[6], (CELLS_ALONG_X, CELLS_ALONG_Y), third_random_key, 2 * third_random_key), jax.random.randint(random_child_keys[7], (CELLS_ALONG_X, CELLS_ALONG_Y), 0, third_random_key))
    sudden_rate_y = jax.random.randint(random_child_keys[8], (CELLS_ALONG_X, CELLS_ALONG_Y), 0, CELLS_ALONG_Y) < 2
    length_class_y = jnp.where(sudden_rate_y, jax.random.randint(random_child_keys[9], (CELLS_ALONG_X, CELLS_ALONG_Y), 2 * third_random_key, SCALE_CLASSES), baseline_rate_y)
    return jnp.stack([length_class_x, length_class_y]).astype(jnp.int32)


def draw_rate_table(key, part):
    random_child_keys = jax.random.split(key, 3)
    third_random_key = SCALE_CLASSES // 3
    length = jnp.array([[float(CELLS_ALONG_X)], [float(CELLS_ALONG_Y)]], jnp.float32)
    gradual_decay_rates = jnp.exp(jax.random.uniform(random_child_keys[0], (2, third_random_key), jnp.float32, jnp.log(0.3), jnp.log(2.0))) / length
    quick_decay_rates = jnp.exp(jax.random.uniform(random_child_keys[1], (2, third_random_key), jnp.float32, jnp.log(0.02), jnp.log(0.033)))
    sudden_rate_values = jax.random.uniform(random_child_keys[2], (2, third_random_key), jnp.float32, 0.2, 0.4)
    return jnp.concatenate([gradual_decay_rates, quick_decay_rates, sudden_rate_values], axis=1).astype(jnp.float32)


def plant(drawn, rng, smallest, largest):
    index_at = [jax.random.randint(jax.random.fold_in(rng, axis), (), 0, length) for axis, length in enumerate(drawn.shape)]
    main_axis = drawn.shape.index(max(drawn.shape))
    neighbour = index_at[:main_axis] + [(index_at[main_axis] + 1) % drawn.shape[main_axis]] + index_at[main_axis + 1:]
    return drawn.at[tuple(index_at)].set(smallest).at[tuple(neighbour)].set(largest)


def level_of(rng, dims, pieces, least, top_value):
    def one(position, parts):
        heights = jax.random.uniform(jax.random.fold_in(jax.random.fold_in(rng, 6), position), (parts,), jnp.float32, least / len(pieces), top_value / len(pieces))
        return jnp.repeat(jnp.exp(heights), dims[position] // parts).reshape((-1,) + (1,) * (len(dims) - position - 1))

    factor_of = one(*pieces[0])
    for cut in pieces[1:]:
        factor_of = factor_of * one(*cut)
    return factor_of


def centred(own_key, extent, scale, most, cuts=(), held_as=jnp.bfloat16):
    entries = jax.random.normal(own_key, extent, jnp.float32) * scale
    if len(cuts) > 0:
        entries = level_of(own_key, extent, cuts, -0.22, 0.18) * entries
    return jnp.clip(entries, min=-most, max=most).astype(held_as)


def setup_inputs(seed: int = 0) -> dict:
    streams_of = jax.random.split(jax.random.key(seed), 13)
    control = centred(streams_of[0], (CELLS_ALONG_X, CELLS_ALONG_Y), 1.0, 6.0, ((0, 8), (1, 4)), jnp.float32)
    background_std = jnp.clip(1.0 + 0.18 * jax.random.normal(streams_of[1], (CELLS_ALONG_X, CELLS_ALONG_Y), jnp.float32), 0.1, 1.9)
    class_index = draw_class_index(jax.random.fold_in(streams_of[12], 71), 0)
    rate_table = draw_rate_table(jax.random.fold_in(streams_of[12], 71), 0)
    brightness = jnp.clip(0.9 * jax.random.uniform(streams_of[4], (2, SUBHOURS), jnp.float32) ** level_of(streams_of[4], (2, SUBHOURS), ((1, 8),), -0.2, 0.2), 0.0, 0.9)
    circumsolar = jnp.clip(3.0 * jax.random.uniform(streams_of[5], (SUBHOURS, ORIENT), jnp.float32) ** level_of(streams_of[5], (SUBHOURS, ORIENT), ((0, 8),), -0.2, 0.2), 0.0, 3.0)
    isotropic = jnp.clip(jax.random.uniform(streams_of[6], (ORIENT,), jnp.float32, 0.5, 1.0), 0.5, 1.0)
    horizon = jnp.clip(jax.random.uniform(streams_of[7], (ORIENT,), jnp.float32, 0.0, 1.0), 0.0, 1.0)
    obs_cell = plant(jax.random.randint(streams_of[8], (N_GX, N_GY, OBS_DEV), 0, CX * CY), jax.random.fold_in(streams_of[8], 1), 0, (CX * CY) - 1).astype(jnp.int32)
    obs_subhour = plant(jax.random.randint(streams_of[9], (N_GX, N_GY, OBS_DEV), 0, SUBHOURS), jax.random.fold_in(streams_of[9], 1), 0, SUBHOURS - 1).astype(jnp.int32)
    obs_orient = plant(jax.random.randint(streams_of[10], (N_GX, N_GY, OBS_DEV), 0, ORIENT), jax.random.fold_in(streams_of[10], 1), 0, ORIENT - 1).astype(jnp.int32)
    obs_value = centred(streams_of[11], (N_GX, N_GY, OBS_DEV), 1.0, 6.0, ((0, 8), (1, 4)), jnp.float32)
    return {"control": control, "background_std": background_std, "class_index": class_index, "rate_table": rate_table, "brightness": brightness, "circumsolar": circumsolar, "isotropic": isotropic, "horizon": horizon, "obs_cell": obs_cell, "obs_subhour": obs_subhour, "obs_orient": obs_orient, "obs_value": obs_value}


def scan_section(decay_rate, source, reverse):

    def advance(current, inputs):
        current = inputs[0] * current + inputs[1]
        return (current, current)
    start = jnp.zeros(decay_rate.shape[1:], jnp.float32)
    _, outputs = lax.scan(advance, start, (decay_rate, source), reverse=reverse)
    return outputs

def cascade_lines(rates, source, reverse):
    decay_rate = 1.0 - rates
    current = source
    for section_no in range(4):
        current = scan_section(decay_rate, rates * current, reverse)
    return current

def reference(control, background_std, class_index, rate_table, brightness, circumsolar, isotropic, horizon, obs_cell, obs_subhour, obs_orient, obs_value):
    rate_x = rate_table[0][class_index[0]]
    rate_y = rate_table[1][class_index[1]]
    spread = control * background_std * lax.rsqrt(rate_x)
    smooth_x = cascade_lines(rate_x, cascade_lines(rate_x, spread, False), True)
    scaled = (smooth_x * lax.rsqrt(rate_y)).T
    rate_t = rate_y.T
    smooth_y = cascade_lines(rate_t, cascade_lines(rate_t, scaled, False), True).T
    increment = background_std * (control + smooth_y)
    factor = (1.0 - brightness[0][:, None]) * isotropic[None, :] + brightness[0][:, None] * circumsolar + brightness[1][:, None] * horizon[None, :]
    tile_x = jnp.arange(N_GX, dtype=jnp.int32)[:, None, None]
    tile_y = jnp.arange(N_GY, dtype=jnp.int32)[None, :, None]
    global_x = tile_x * CX + obs_cell // CY
    global_y = tile_y * CY + obs_cell % CY
    values = increment[global_x, global_y]
    factors = factor[obs_subhour, obs_orient]
    departure = obs_value - factors * values
    return (increment, departure)
```

```python
import jax
import jax.numpy as jnp
from jax import lax
from jax.experimental import pallas as pl
from jax.experimental.pallas import tpu as pltpu
from jax.sharding import PartitionSpec as P

LANES = 128
ROWS = 8
TILES = 3
Y_BLOCKS = 8


def iota(axis):
    return lax.broadcasted_iota(jnp.int32, (ROWS, LANES), axis)


def pack_kernel(sources, halves, quarters, parts):
    def body(bright, table, control, std, classes, circumsolar, isotropic, horizon, payload, own, rates):
        place_x = lax.axis_index("gx")
        place_y = lax.axis_index("gy")
        kinds, entries = table.shape
        rates[0:kinds, 0:entries] = table[...]
        rate = [
            jnp.take_along_axis(rates[pl.ds(which, ROWS, stride=0), :], classes[which], axis=1)
            for which in range(2)
        ]
        spread = control[...] * std[...] * lax.rsqrt(rate[0])
        hours = ROWS // parts
        row = iota(0)
        for quarter in range(quarters):
            first = jnp.zeros((ROWS, LANES), jnp.float32)
            second = first
            sky = first
            sine = first
            sun = first
            for part in range(parts):
                here = (row >= part * hours) & (row < (part + 1) * hours)
                sky = jnp.where(here, jnp.broadcast_to(isotropic[part : part + 1, :], (ROWS, LANES)), sky)
                sine = jnp.where(here, jnp.broadcast_to(horizon[part : part + 1, :], (ROWS, LANES)), sine)
                for hour in range(hours):
                    at = quarter * hours + hour
                    this = row == part * hours + hour
                    first = jnp.where(this, bright[0, at], first)
                    second = jnp.where(this, bright[1, at], second)
                    sun = jnp.where(
                        this,
                        jnp.broadcast_to(
                            circumsolar[at : at + 1, part * LANES : (part + 1) * LANES], (ROWS, LANES)
                        ),
                        sun,
                    )
            own[quarter] = (1.0 - first) * sky + first * sun + second * sine
        mine = own[place_y]

        def fill(target, carry):
            payload[target, 0] = spread
            payload[target, 1] = rate[0]
            payload[target, 2] = mine
            return carry

        lax.fori_loop(0, sources, fill, 0, unroll=sources if sources <= 16 else 1)
        for half in range(halves):
            payload[place_x * halves + half, 2] = rate[1]

    return body


def advance(states, keep, rate, source):
    states = list(states)
    for section in range(4):
        gain = rate * source if source is not None else None
        states[section] = keep * states[section] + gain if gain is not None else keep * states[section]
        source = states[section]
    return tuple(states)


def log2(size):
    assert size & (size - 1) == 0
    return size.bit_length() - 1


def main_kernel(count_x, columns, cell_y, parts):
    steps = columns * cell_y // Y_BLOCKS
    block_rows = TILES * ROWS
    group_rows = columns * block_rows

    def body(
        near, far, own, control, std, obs_cell, obs_subhour, obs_orient, obs_value,
        increment, departure,
        field, ahead, smooth, source, rate, answer, free, impulse, sems,
    ):
        place_x = lax.axis_index("gx")
        place_y = lax.axis_index("gy")
        core = place_y % 2
        copies = [
            pltpu.make_async_copy(near, field.at[:, core], sems.at[0]),
            pltpu.make_async_copy(far, field.at[:, 1 - core], sems.at[1]),
        ]
        for copy in copies:
            copy.start()
        for copy in copies:
            copy.wait()
        flat = field.reshape(count_x * group_rows, LANES)

        rates_y = []
        for column in range(columns):
            at = place_x * columns + column
            tile = flat[pl.ds(pl.multiple_of(at * block_rows + 2 * ROWS, ROWS), ROWS), :]
            rates_y.append(tile)
            rate[column * cell_y : (column + 1) * cell_y, 0:ROWS] = tile.T
        for column in range(columns):
            at = place_x * columns + column
            flat[pl.ds(pl.multiple_of(at * block_rows + 2 * ROWS, ROWS), ROWS), :] = own[column]

        def cells(group, row, tile):
            return flat[pl.ds(group * group_rows + tile * ROWS + row, columns, stride=block_rows), :]

        still = (jnp.zeros((columns, LANES), jnp.float32),) * 4

        def forward(group, states):
            for row in range(ROWS):
                q = cells(group, row, 1)
                states = advance(states, 1.0 - q, q, cells(group, row, 0))
                ahead[pl.ds((group * ROWS + row) * columns, columns), :] = states[3]
            return states

        def backward(turn, states):
            group = count_x - 1 - turn
            for row in range(ROWS - 1, -1, -1):
                q = cells(group, row, 1)
                at = (group * ROWS + row) * columns
                states = advance(states, 1.0 - q, q, ahead[pl.ds(at, columns), :])
                smooth[pl.ds(at, columns), :] = states[3]
            return states

        unroll = count_x if count_x <= 8 else 1
        lax.fori_loop(0, count_x, forward, still, unroll=unroll)
        lax.fori_loop(0, count_x, backward, still, unroll=unroll)

        for column in range(columns):
            tile = smooth[pl.ds(place_x * ROWS * columns + column, ROWS, stride=columns), :]
            scaled = tile * lax.rsqrt(rates_y[column])
            source[column * cell_y : (column + 1) * cell_y, 0:ROWS] = scaled.T

        nothing = jnp.zeros((ROWS, LANES), jnp.float32)
        sublane = iota(0)

        def line(given, result, reverse):
            order = range(steps - 1, -1, -1) if reverse else range(steps)
            states = (nothing,) * 4
            unit = (nothing + 1.0, nothing, nothing, nothing)
            for step in order:
                at = pl.ds(step, Y_BLOCKS, stride=steps)
                q = rate[at, :]
                keep = 1.0 - q
                states = advance(states, keep, q, given[at, :])
                unit = advance(unit, keep, q, None)
                free[step] = states[3]
                for section in range(4):
                    impulse[section, step] = unit[section]
            entering = [nothing] * 4
            state = [nothing] * 4
            blocks = range(Y_BLOCKS - 1, -1, -1) if reverse else range(Y_BLOCKS)

            def row_of(value, block):
                return jnp.broadcast_to(value[block : block + 1, :], (ROWS, LANES))

            for block in blocks:
                entering = [jnp.where(sublane == block, s, e) for s, e in zip(state, entering)]
                response = [row_of(u, block) for u in unit]
                offset = [row_of(s, block) for s in states]
                fresh = []
                for section in range(4):
                    total = offset[section]
                    for lower in range(section + 1):
                        total = total + response[section - lower] * state[lower]
                    fresh.append(total)
                state = fresh
            for step in range(steps):
                total = free[step]
                for section in range(4):
                    total = total + impulse[3 - section, step] * entering[section]
                result[pl.ds(step, Y_BLOCKS, stride=steps), :] = total

        line(source, answer, False)
        line(answer, source, True)
        smooth_y = source[pl.ds(pl.multiple_of(place_y * cell_y, cell_y), cell_y), :].T[0:ROWS]
        change = std[...] * (control[...] + smooth_y)
        increment[...] = change

        hour = obs_subhour[...]
        orient = obs_orient[...]
        span = ROWS // parts
        key = ((hour >> log2(span)) << log2(ROWS)) + ((orient >> log2(LANES)) << log2(span)) + (hour & (span - 1))
        lane = orient & (LANES - 1)

        def scan_rows(block, factors):
            for row in range(ROWS):
                values = flat[pl.ds(block * block_rows + 2 * ROWS + row, ROWS, stride=0), :]
                picked = jnp.take_along_axis(values, lane, axis=1)
                factors = jnp.where(key == block * ROWS + row, picked, factors)
            return factors

        blocks_in_all = count_x * columns
        factors = lax.fori_loop(
            0, blocks_in_all, scan_rows, nothing, unroll=blocks_in_all if blocks_in_all <= 32 else 1
        )
        cell = obs_cell[...]
        cell_lane = cell & (LANES - 1)
        cell_row = cell >> log2(LANES)
        values = nothing
        for row in range(ROWS):
            picked = jnp.take_along_axis(
                jnp.broadcast_to(change[row : row + 1, :], (ROWS, LANES)), cell_lane, axis=1
            )
            values = jnp.where(cell_row == row, picked, values)
        departure[...] = obs_value[...] - factors * values

    return body


def spec(space=pltpu.VMEM):
    return pl.BlockSpec(memory_space=space)


def array(*shape):
    return jax.ShapeDtypeStruct(shape, jnp.float32)


def solution(mesh):
    count_x = mesh.shape["gx"]
    columns = mesh.shape["gy"]
    halves = columns // 2
    sources = count_x * halves
    groups = [
        [place * columns + 2 * half + core for place in range(count_x) for half in range(halves)]
        for core in range(2)
    ]
    swap = [(place, place ^ 1) for place in range(columns)]

    def on_device(
        control,
        background_std,
        class_index,
        rate_table,
        brightness,
        circumsolar,
        isotropic,
        horizon,
        obs_cell,
        obs_subhour,
        obs_orient,
        obs_value,
    ):
        cell_x, cell_y = control.shape
        hours, orients = circumsolar.shape
        parts = orients // LANES
        assert (cell_x, cell_y) == (ROWS, LANES) and hours * parts == ROWS * columns
        assert obs_value.size == ROWS * LANES
        payload, own = pl.pallas_call(
            pack_kernel(sources, halves, columns, parts),
            out_shape=(array(sources, TILES, ROWS, LANES), array(columns, ROWS, LANES)),
            in_specs=[spec(pltpu.SMEM)] + [spec()] * 7,
            out_specs=(spec(), spec()),
            scratch_shapes=[pltpu.VMEM((ROWS, LANES), jnp.float32)],
            name="pack",
        )(
            brightness,
            rate_table,
            control,
            background_std,
            class_index,
            circumsolar,
            isotropic.reshape(parts, LANES),
            horizon.reshape(parts, LANES),
        )
        near = lax.all_to_all(payload, ("gx", "gy"), 0, 0, axis_index_groups=groups, tiled=True)
        far = lax.ppermute(near, "gy", swap)
        whole_y = columns * cell_y
        steps = whole_y // Y_BLOCKS
        increment, departure = pl.pallas_call(
            main_kernel(count_x, columns, cell_y, parts),
            out_shape=(array(ROWS, LANES), array(ROWS, LANES)),
            in_specs=[spec(pl.ANY)] * 2 + [spec()] * 7,
            out_specs=(spec(), spec()),
            scratch_shapes=[
                pltpu.VMEM((sources, 2, TILES, ROWS, LANES), jnp.float32),
                pltpu.VMEM((count_x * ROWS * columns, LANES), jnp.float32),
                pltpu.VMEM((count_x * ROWS * columns, LANES), jnp.float32),
                pltpu.VMEM((whole_y, LANES), jnp.float32),
                pltpu.VMEM((whole_y, LANES), jnp.float32),
                pltpu.VMEM((whole_y, LANES), jnp.float32),
                pltpu.VMEM((steps, Y_BLOCKS, LANES), jnp.float32),
                pltpu.VMEM((4, steps, Y_BLOCKS, LANES), jnp.float32),
                pltpu.SemaphoreType.DMA((2,)),
            ],
            name="main",
        )(
            near,
            far,
            own,
            control,
            background_std,
            *[a.reshape(ROWS, LANES) for a in (obs_cell, obs_subhour, obs_orient, obs_value)],
        )
        return increment, departure.reshape(obs_value.shape)

    in_specs = (
        P("gx", "gy"),
        P("gx", "gy"),
        P(None, "gx", "gy"),
        P(),
        P(None, "gx"),
        P("gx", None),
        P(),
        P(),
        P("gx", "gy", None),
        P("gx", "gy", None),
        P("gx", "gy", None),
        P("gx", "gy", None),
    )
    out_specs = (P("gx", "gy"), P("gx", "gy", None))
    return jax.shard_map(
        on_device, mesh=mesh, in_specs=in_specs, out_specs=out_specs, check_vma=False
    )
```

```python
import jax
import jax.numpy as jnp
from jax import lax
from jax.experimental import pallas as pl
from jax.experimental.pallas import tpu as pltpu
from jax.sharding import PartitionSpec as P

LANES = 128
ROWS = 8
TILES = 3
Y_BLOCKS = 8


def iota(axis):
    return lax.broadcasted_iota(jnp.int32, (ROWS, LANES), axis)


def pack_kernel(sources, halves, quarters, parts):
    def body(bright, table, control, std, classes, circumsolar, isotropic, horizon, payload, own, fields, rates):
        place_x = lax.axis_index("gx")
        place_y = lax.axis_index("gy")
        kinds, entries = table.shape
        rates[0:kinds, 0:entries] = table[...]
        rate = [
            jnp.take_along_axis(rates[pl.ds(which, ROWS, stride=0), :], classes[which], axis=1)
            for which in range(2)
        ]
        fields[0] = control[...]
        fields[1] = std[...]
        spread = control[...] * std[...] * lax.rsqrt(rate[0])
        hours = ROWS // parts
        row = iota(0)
        for quarter in range(quarters):
            first = jnp.zeros((ROWS, LANES), jnp.float32)
            second = first
            sky = first
            sine = first
            sun = first
            for part in range(parts):
                here = (row >= part * hours) & (row < (part + 1) * hours)
                sky = jnp.where(here, jnp.broadcast_to(isotropic[part : part + 1, :], (ROWS, LANES)), sky)
                sine = jnp.where(here, jnp.broadcast_to(horizon[part : part + 1, :], (ROWS, LANES)), sine)
                for hour in range(hours):
                    at = quarter * hours + hour
                    this = row == part * hours + hour
                    first = jnp.where(this, bright[0, at], first)
                    second = jnp.where(this, bright[1, at], second)
                    sun = jnp.where(
                        this,
                        jnp.broadcast_to(
                            circumsolar[at : at + 1, part * LANES : (part + 1) * LANES], (ROWS, LANES)
                        ),
                        sun,
                    )
            own[quarter] = (1.0 - first) * sky + first * sun + second * sine
        mine = own[place_y]

        def fill(target, carry):
            payload[target, 0] = spread
            payload[target, 1] = rate[0]
            payload[target, 2] = mine
            return carry

        lax.fori_loop(0, sources, fill, 0, unroll=sources if sources <= 16 else 1)
        for half in range(halves):
            payload[place_x * halves + half, 2] = rate[1]

    return body


def advance(states, keep, rate, source):
    states = list(states)
    for section in range(4):
        gain = rate * source if source is not None else None
        states[section] = keep * states[section] + gain if gain is not None else keep * states[section]
        source = states[section]
    return tuple(states)


def log2(size):
    assert size & (size - 1) == 0
    return size.bit_length() - 1


def main_kernel(count_x, columns, cell_y, parts):
    steps = columns * cell_y // Y_BLOCKS
    block_rows = TILES * ROWS
    group_rows = columns * block_rows

    def body(
        near, far, own, fields, cells_hbm, subhours_hbm, orients_hbm, values_hbm,
        increment, departure,
        field, ahead, smooth, source, rate, answer, free, impulse,
        obs_cell, obs_subhour, obs_orient, obs_value, arrived,
    ):
        fetches = [
            pltpu.make_async_copy(given, held, arrived.at[which])
            for which, (given, held) in enumerate(
                [
                    (cells_hbm, obs_cell),
                    (subhours_hbm, obs_subhour),
                    (orients_hbm, obs_orient),
                    (values_hbm, obs_value),
                ]
            )
        ]
        for fetch in fetches:
            fetch.start()
        place_x = lax.axis_index("gx")
        place_y = lax.axis_index("gy")
        core = place_y % 2
        whole = count_x * columns // 2 <= 16
        piece = count_x * columns // 2 if whole else 1

        def place(at, carry):
            field[pl.ds(at * piece, piece), core] = near[pl.ds(at * piece, piece)]
            field[pl.ds(at * piece, piece), 1 - core] = far[pl.ds(at * piece, piece)]
            return carry

        lax.fori_loop(0, count_x * columns // 2 // piece, place, 0, unroll=whole)
        flat = field.reshape(count_x * group_rows, LANES)

        rates_y = []
        for column in range(columns):
            at = place_x * columns + column
            tile = flat[pl.ds(pl.multiple_of(at * block_rows + 2 * ROWS, ROWS), ROWS), :]
            rates_y.append(tile)
            rate[column * cell_y : (column + 1) * cell_y, 0:ROWS] = tile.T
        for column in range(columns):
            at = place_x * columns + column
            flat[pl.ds(pl.multiple_of(at * block_rows + 2 * ROWS, ROWS), ROWS), :] = own[column]

        def cells(group, row, tile):
            return flat[pl.ds(group * group_rows + tile * ROWS + row, columns, stride=block_rows), :]

        still = (jnp.zeros((columns, LANES), jnp.float32),) * 4

        def forward(group, states):
            for row in range(ROWS):
                q = cells(group, row, 1)
                states = advance(states, 1.0 - q, q, cells(group, row, 0))
                ahead[pl.ds((group * ROWS + row) * columns, columns), :] = states[3]
            return states

        def backward(turn, states):
            group = count_x - 1 - turn
            for row in range(ROWS - 1, -1, -1):
                q = cells(group, row, 1)
                at = (group * ROWS + row) * columns
                states = advance(states, 1.0 - q, q, ahead[pl.ds(at, columns), :])
                smooth[pl.ds(at, columns), :] = states[3]
            return states

        unroll = count_x if count_x <= 8 else 1
        lax.fori_loop(0, count_x, forward, still, unroll=unroll)
        lax.fori_loop(0, count_x, backward, still, unroll=unroll)

        for column in range(columns):
            tile = smooth[pl.ds(place_x * ROWS * columns + column, ROWS, stride=columns), :]
            scaled = tile * lax.rsqrt(rates_y[column])
            source[column * cell_y : (column + 1) * cell_y, 0:ROWS] = scaled.T

        nothing = jnp.zeros((ROWS, LANES), jnp.float32)
        sublane = iota(0)

        def line(given, result, reverse):
            order = range(steps - 1, -1, -1) if reverse else range(steps)
            states = (nothing,) * 4
            unit = (nothing + 1.0, nothing, nothing, nothing)
            for step in order:
                at = pl.ds(step, Y_BLOCKS, stride=steps)
                q = rate[at, :]
                keep = 1.0 - q
                states = advance(states, keep, q, given[at, :])
                unit = advance(unit, keep, q, None)
                free[step] = states[3]
                for section in range(4):
                    impulse[section, step] = unit[section]
            entering = [nothing] * 4
            state = [nothing] * 4
            blocks = range(Y_BLOCKS - 1, -1, -1) if reverse else range(Y_BLOCKS)

            def row_of(value, block):
                return jnp.broadcast_to(value[block : block + 1, :], (ROWS, LANES))

            for block in blocks:
                entering = [jnp.where(sublane == block, s, e) for s, e in zip(state, entering)]
                response = [row_of(u, block) for u in unit]
                offset = [row_of(s, block) for s in states]
                fresh = []
                for section in range(4):
                    total = offset[section]
                    for lower in range(section + 1):
                        total = total + response[section - lower] * state[lower]
                    fresh.append(total)
                state = fresh
            for step in range(steps):
                total = free[step]
                for section in range(4):
                    total = total + impulse[3 - section, step] * entering[section]
                result[pl.ds(step, Y_BLOCKS, stride=steps), :] = total

        line(source, answer, False)
        line(answer, source, True)
        smooth_y = source[pl.ds(pl.multiple_of(place_y * cell_y, cell_y), cell_y), :].T[0:ROWS]
        change = fields[1] * (fields[0] + smooth_y)
        increment[...] = change

        for fetch in fetches:
            fetch.wait()
        hour = obs_subhour[...]
        orient = obs_orient[...]
        span = ROWS // parts
        key = ((hour >> log2(span)) << log2(ROWS)) + ((orient >> log2(LANES)) << log2(span)) + (hour & (span - 1))
        lane = orient & (LANES - 1)

        def scan_rows(block, factors):
            for row in range(ROWS):
                values = flat[pl.ds(block * block_rows + 2 * ROWS + row, ROWS, stride=0), :]
                picked = jnp.take_along_axis(values, lane, axis=1)
                factors = jnp.where(key == block * ROWS + row, picked, factors)
            return factors

        blocks_in_all = count_x * columns
        factors = lax.fori_loop(
            0, blocks_in_all, scan_rows, nothing, unroll=blocks_in_all if blocks_in_all <= 32 else 1
        )
        cell = obs_cell[...]
        cell_lane = cell & (LANES - 1)
        cell_row = cell >> log2(LANES)
        values = nothing
        for row in range(ROWS):
            picked = jnp.take_along_axis(
                jnp.broadcast_to(change[row : row + 1, :], (ROWS, LANES)), cell_lane, axis=1
            )
            values = jnp.where(cell_row == row, picked, values)
        departure[...] = obs_value[...] - factors * values

    return body


def spec(space=pltpu.VMEM):
    return pl.BlockSpec(memory_space=space)


def array(*shape):
    return jax.ShapeDtypeStruct(shape, jnp.float32)


def on_chip(*arrays):
    return [pltpu.with_memory_space_constraint(a, pltpu.VMEM) for a in arrays]


def solution(mesh):
    count_x = mesh.shape["gx"]
    columns = mesh.shape["gy"]
    halves = columns // 2
    sources = count_x * halves
    groups = [
        [place * columns + 2 * half + core for place in range(count_x) for half in range(halves)]
        for core in range(2)
    ]
    swap = [(place, place ^ 1) for place in range(columns)]

    def on_device(
        control,
        background_std,
        class_index,
        rate_table,
        brightness,
        circumsolar,
        isotropic,
        horizon,
        obs_cell,
        obs_subhour,
        obs_orient,
        obs_value,
    ):
        cell_x, cell_y = control.shape
        hours, orients = circumsolar.shape
        parts = orients // LANES
        assert (cell_x, cell_y) == (ROWS, LANES) and hours * parts == ROWS * columns
        assert obs_value.size == ROWS * LANES
        payload, own, fields = pl.pallas_call(
            pack_kernel(sources, halves, columns, parts),
            out_shape=(
                pltpu.VMEM((sources, TILES, ROWS, LANES), jnp.float32),
                pltpu.VMEM((columns, ROWS, LANES), jnp.float32),
                pltpu.VMEM((2, ROWS, LANES), jnp.float32),
            ),
            in_specs=[spec(pltpu.SMEM)] + [spec()] * 7,
            out_specs=(spec(),) * 3,
            scratch_shapes=[pltpu.VMEM((ROWS, LANES), jnp.float32)],
            name="pack",
        )(
            brightness,
            rate_table,
            control,
            background_std,
            class_index,
            circumsolar,
            isotropic.reshape(parts, LANES),
            horizon.reshape(parts, LANES),
        )
        near = lax.all_to_all(payload, ("gx", "gy"), 0, 0, axis_index_groups=groups, tiled=True)
        far = lax.ppermute(near, "gy", swap)
        whole_y = columns * cell_y
        steps = whole_y // Y_BLOCKS
        increment, departure = pl.pallas_call(
            main_kernel(count_x, columns, cell_y, parts),
            out_shape=(array(ROWS, LANES), array(ROWS, LANES)),
            in_specs=[spec()] * 4 + [spec(pl.ANY)] * 4,
            out_specs=(spec(), spec()),
            scratch_shapes=[
                pltpu.VMEM((sources, 2, TILES, ROWS, LANES), jnp.float32),
                pltpu.VMEM((count_x * ROWS * columns, LANES), jnp.float32),
                pltpu.VMEM((count_x * ROWS * columns, LANES), jnp.float32),
                pltpu.VMEM((whole_y, LANES), jnp.float32),
                pltpu.VMEM((whole_y, LANES), jnp.float32),
                pltpu.VMEM((whole_y, LANES), jnp.float32),
                pltpu.VMEM((steps, Y_BLOCKS, LANES), jnp.float32),
                pltpu.VMEM((4, steps, Y_BLOCKS, LANES), jnp.float32),
                pltpu.VMEM((ROWS, LANES), jnp.int32),
                pltpu.VMEM((ROWS, LANES), jnp.int32),
                pltpu.VMEM((ROWS, LANES), jnp.int32),
                pltpu.VMEM((ROWS, LANES), jnp.float32),
                pltpu.SemaphoreType.DMA((4,)),
            ],
            name="main",
        )(
            *on_chip(near, far, own, fields),
            *[a.reshape(ROWS, LANES) for a in (obs_cell, obs_subhour, obs_orient, obs_value)],
        )
        return increment, departure.reshape(obs_value.shape)

    in_specs = (
        P("gx", "gy"),
        P("gx", "gy"),
        P(None, "gx", "gy"),
        P(),
        P(None, "gx"),
        P("gx", None),
        P(),
        P(),
        P("gx", "gy", None),
        P("gx", "gy", None),
        P("gx", "gy", None),
        P("gx", "gy", None),
    )
    out_specs = (P("gx", "gy"), P("gx", "gy", None))
    return jax.shard_map(
        on_device, mesh=mesh, in_specs=in_specs, out_specs=out_specs, check_vma=False
    )
```

```python
import jax
import jax.numpy as jnp
from jax import lax
from jax.experimental import pallas as pl
from jax.experimental.pallas import tpu as pltpu
from jax.sharding import PartitionSpec as P

LANES = 128
ROWS = 8
TILES = 3
Y_BLOCKS = 8
PAD = 8


def iota(axis):
    return lax.broadcasted_iota(jnp.int32, (ROWS, LANES), axis)


def log2(size):
    assert size & (size - 1) == 0
    return size.bit_length() - 1


def spread_row(row):
    return jnp.broadcast_to(row, (ROWS, LANES))


def split(wide, pieces):
    for part in range(pieces.shape[0]):
        pieces[part] = wide[:, part * LANES : (part + 1) * LANES]


def factor_tile(first_hour, parts, bright, ratios, isotropic, horizon):
    hours = ROWS // parts
    row = iota(0)
    near_sun = jnp.zeros((ROWS, LANES), jnp.float32)
    near_edge = near_sun
    sky = near_sun
    sine = near_sun
    sun = near_sun
    for part in range(parts):
        here = row >= part * hours
        sky = jnp.where(here, spread_row(isotropic[part : part + 1, :]), sky)
        sine = jnp.where(here, spread_row(horizon[part : part + 1, :]), sine)
        for hour in range(hours):
            at = first_hour + hour
            this = row == part * hours + hour
            near_sun = jnp.where(this, bright[0, at], near_sun)
            near_edge = jnp.where(this, bright[1, at], near_edge)
            ratio = ratios[part, pl.ds(at, 1), :]
            sun = jnp.where(this, spread_row(ratio), sun)
    return (1.0 - near_sun) * sky + near_sun * sun + near_edge * sine


def pack_kernel(chips, halves, parts):
    def body(bright, table, control, std, classes, circumsolar, isotropic, horizon, payload, fields, rates, ratios):
        place_x = lax.axis_index("gx")
        place_y = lax.axis_index("gy")
        kinds, entries = table.shape
        rates[0:kinds, 0:entries] = table[...]
        rate = [
            jnp.take_along_axis(rates[pl.ds(which, ROWS, stride=0), :], classes[which], axis=1)
            for which in range(2)
        ]
        fields[0] = control[...]
        fields[1] = std[...]
        spread = control[...] * std[...] * lax.rsqrt(rate[0])
        split(circumsolar, ratios)
        mine = factor_tile(place_y * (ROWS // parts), parts, bright, ratios, isotropic, horizon)

        half = ROWS // 2
        blocks = [
            [
                jnp.concatenate([spread[:half], rate[0][:half]], 0),
                jnp.concatenate([third[:half], spread[half:]], 0),
                jnp.concatenate([rate[0][half:], third[half:]], 0),
            ]
            for third in (mine, rate[1])
        ]

        def put(chip, tiles):
            at = pl.multiple_of(chip * TILES * ROWS, ROWS)
            for tile in range(TILES):
                payload[pl.ds(at + tile * ROWS, ROWS), :] = tiles[tile]

        def fill(chip, carry):
            put(chip, blocks[0])
            return carry

        lax.fori_loop(0, chips, fill, 0, unroll=chips if chips <= 16 else 1)
        for chip in range(halves):
            put(place_x * halves + chip, blocks[1])

    return body


def look_rows(tiles, sources, keys, lane, factors):
    height = ROWS // 2

    def scan(source, factors):
        for row in range(height):
            values = tiles[pl.ds((source * TILES + 2) * height + row, ROWS, stride=0), :]
            picked = jnp.take_along_axis(values, lane, axis=1)
            factors = jnp.where(keys == source * height + row, picked, factors)
        return factors

    return lax.fori_loop(0, sources, scan, factors, unroll=sources if sources <= 32 else 1)


def look_kernel(sources, hours):
    def body(
        bright, near, circumsolar, isotropic, horizon, obs_cell, obs_subhour, obs_orient, obs_value,
        indices, partial,
    ):
        place_x = lax.axis_index("gx")
        core = lax.axis_index("gy") % 2
        hour = obs_subhour[...]
        orient = obs_orient[...]
        lane = orient & (LANES - 1)
        part_of = orient >> log2(LANES)
        home = hour - place_x * hours
        at_home = (home >= 0) & (home < hours)
        nothing = jnp.zeros((ROWS, LANES), jnp.float32)
        factors = look_rows(near, sources, jnp.where(part_of == core, hour, -1), lane, nothing)
        row = iota(0)
        for first in range(0, hours, ROWS):
            sun = nothing
            edge = nothing
            for step in range(ROWS):
                sun = jnp.where(row == step, bright[0, first + step], sun)
                edge = jnp.where(row == step, bright[1, first + step], edge)
            for part in range(2):
                ratio = circumsolar[first : first + ROWS, part * LANES : (part + 1) * LANES]
                tile = (
                    (1.0 - sun) * spread_row(isotropic[part : part + 1, :])
                    + sun * ratio
                    + edge * spread_row(horizon[part : part + 1, :])
                )
                keys = jnp.where(part_of == part, home - first, -1)
                for step in range(ROWS):
                    picked = jnp.take_along_axis(spread_row(tile[step : step + 1, :]), lane, axis=1)
                    factors = jnp.where(keys == step, picked, factors)
        indices[0] = jnp.where((part_of == core) | at_home, -1, hour)
        indices[1] = lane
        indices[2] = obs_cell[...]
        partial[0] = factors
        partial[1] = obs_value[...]

    return body


def advance(states, keep, rate, source):
    states = list(states)
    for section in range(4):
        states[section] = keep * states[section] + rate * source
        source = states[section]
    return tuple(states)


def combine(response, state):
    result = []
    for section in range(4):
        total = response[section] * state[0]
        for lower in range(1, section + 1):
            total = total + response[section - lower] * state[lower]
        result.append(total)
    return result


def main_kernel(count_x, columns, cell_y):
    steps = columns * cell_y // Y_BLOCKS
    pieces = Y_BLOCKS // columns
    pitch = steps + PAD
    height = ROWS // 2
    source_rows = TILES * height
    group_rows = columns * source_rows
    rows_in_all = count_x * group_rows

    def body(near, far, fields, indices, partial, increment, departure, field, ahead, smooth, source, rate, answer):
        place_x = lax.axis_index("gx")
        place_y = lax.axis_index("gy")
        core = place_y % 2
        pieces_in_all = 16 if rows_in_all > 16 * 24 else 1
        chunk = rows_in_all // pieces_in_all

        def place(at, carry):
            rows = pl.ds(pl.multiple_of(at * chunk, ROWS), chunk)
            field[core, rows, :] = near[rows, :]
            field[1 - core, rows, :] = far[rows, :]
            return carry

        lax.fori_loop(0, pieces_in_all, place, 0, unroll=pieces_in_all == 1)

        def put_column(target, column, tile):
            turned = tile.T
            for part in range(pieces):
                at = (column * pieces + part) * pitch
                target[at : at + steps, 0:ROWS] = turned[part * steps : (part + 1) * steps]

        def strided(step):
            return pl.ds(step, Y_BLOCKS, stride=pitch)

        rates_y = []
        for column in range(columns):
            at = column * source_rows + 2 * height
            window = pl.ds(pl.multiple_of(place_x * group_rows + at // ROWS * ROWS, ROWS), ROWS)
            inside = slice(at % ROWS, at % ROWS + height)
            tile = jnp.concatenate([field[0, window, :][inside], field[1, window, :][inside]], 0)
            rates_y.append(tile)
            put_column(rate, column, tile)

        nothing = jnp.zeros((ROWS, LANES), jnp.float32)
        product = nothing + 1.0
        sums = [nothing] * 3
        for step in range(steps):
            q = rate[strided(step), :]
            square = q * q
            product = product * (1.0 - q)
            sums = [sums[0] + q, sums[1] + square, sums[2] + square * q]
        one, two, three = sums
        response = [
            product,
            product * one,
            product * ((one * one + two) * 0.5),
            product * ((one * (one * one + 3.0 * two) + 2.0 * three) * (1.0 / 6.0)),
        ]
        block = iota(0)

        def shift(values, by, hide=False):
            moved = [pltpu.roll(value, by % Y_BLOCKS, 0) for value in values]
            if hide:
                inside = block >= by if by > 0 else block < Y_BLOCKS + by
                moved = [jnp.where(inside, value, 0.0) for value in moved]
            return moved

        pairs = combine(response, shift(response, 1))
        fours = combine(pairs, shift(pairs, 2))
        levels = ((1, response), (2, pairs), (4, fours))
        levels_back = ((1, response), (2, shift(pairs, -1)), (4, shift(fours, -3)))

        def cells(group, row, tile):
            at = group * group_rows + tile * height + row % height
            return field[row // height, pl.ds(at, columns, stride=source_rows), :]

        still = (jnp.zeros((columns, LANES), jnp.float32),) * 4

        def forward(group, states):
            for row in range(ROWS):
                q = cells(group, row, 1)
                states = advance(states, 1.0 - q, q, cells(group, row, 0))
                ahead[pl.ds((group * ROWS + row) * columns, columns), :] = states[3]
            return states

        def backward(turn, states):
            group = count_x - 1 - turn
            for row in range(ROWS - 1, -1, -1):
                q = cells(group, row, 1)
                at = (group * ROWS + row) * columns
                states = advance(states, 1.0 - q, q, ahead[pl.ds(at, columns), :])
                smooth[pl.ds(at, columns), :] = states[3]
            return states

        unroll = count_x if count_x <= 8 else 1
        lax.fori_loop(0, count_x, forward, still, unroll=unroll)
        lax.fori_loop(0, count_x, backward, still, unroll=unroll)

        for column in range(columns):
            tile = smooth[pl.ds(place_x * ROWS * columns + column, ROWS, stride=columns), :]
            put_column(source, column, tile * lax.rsqrt(rates_y[column]))

        def line(given, result, reverse):
            order = range(steps - 1, -1, -1) if reverse else range(steps)
            way = -1 if reverse else 1
            states = (nothing,) * 4
            for step in order:
                q = rate[strided(step), :]
                states = advance(states, 1.0 - q, q, given[strided(step), :])
            for by, maps in levels_back if reverse else levels:
                added = combine(maps, shift(states, way * by, True))
                states = [state + more for state, more in zip(states, added)]
            states = shift(states, way, True)
            for step in order:
                q = rate[strided(step), :]
                states = advance(states, 1.0 - q, q, given[strided(step), :])
                result[strided(step), :] = states[3]

        line(source, answer, False)
        line(answer, source, True)
        own = [source[pl.ds((place_y * pieces + part) * pitch, steps), :] for part in range(pieces)]
        smooth_y = jnp.concatenate(own, 0).T[0:ROWS]
        change = fields[1] * (fields[0] + smooth_y)
        increment[...] = change

        factors = look_rows(far, count_x * columns, indices[0], indices[1], partial[0])
        cell = indices[2]
        cell_lane = cell & (LANES - 1)
        cell_row = cell >> log2(LANES)
        values = nothing
        for row in range(ROWS):
            picked = jnp.take_along_axis(spread_row(change[row : row + 1, :]), cell_lane, axis=1)
            values = jnp.where(cell_row == row, picked, values)
        departure[...] = partial[1] - factors * values

    return body


def spec(space=pltpu.VMEM):
    return pl.BlockSpec(memory_space=space)


def array(*shape):
    return jax.ShapeDtypeStruct(shape, jnp.float32)


def on_chip(*arrays):
    return [pltpu.with_memory_space_constraint(a, pltpu.VMEM) for a in arrays]


def solution(mesh):
    count_x = mesh.shape["gx"]
    columns = mesh.shape["gy"]
    halves = columns // 2
    sources = count_x * columns
    rows_in_all = sources * TILES * ROWS // 2
    swap = [(place, place ^ 1) for place in range(columns)]

    def on_device(
        control,
        background_std,
        class_index,
        rate_table,
        brightness,
        circumsolar,
        isotropic,
        horizon,
        obs_cell,
        obs_subhour,
        obs_orient,
        obs_value,
    ):
        cell_x, cell_y = control.shape
        hours, orients = circumsolar.shape
        parts = orients // LANES
        assert (cell_x, cell_y) == (ROWS, LANES) and parts == 2 and hours * parts == ROWS * columns
        assert obs_value.size == ROWS * LANES
        table = (circumsolar, isotropic.reshape(parts, LANES), horizon.reshape(parts, LANES))
        payload, fields = pl.pallas_call(
            pack_kernel(count_x * halves, halves, parts),
            out_shape=(
                pltpu.VMEM((rows_in_all, LANES), jnp.float32),
                pltpu.VMEM((2, ROWS, LANES), jnp.float32),
            ),
            in_specs=[spec(pltpu.SMEM)] + [spec()] * 7,
            out_specs=(spec(),) * 2,
            scratch_shapes=[pltpu.VMEM((ROWS, LANES), jnp.float32), pltpu.VMEM((parts, hours, LANES), jnp.float32)],
            name="pack",
        )(brightness, rate_table, control, background_std, class_index, *table)
        near = lax.all_to_all(
            payload.reshape(sources, TILES, ROWS // 2, LANES), ("gx", "gy"), 0, 0, tiled=True
        ).reshape(rows_in_all, LANES)
        far = lax.ppermute(near, "gy", swap)
        indices, partial = pl.pallas_call(
            look_kernel(sources, hours),
            out_shape=(
                pltpu.VMEM((3, ROWS, LANES), jnp.int32),
                pltpu.VMEM((2, ROWS, LANES), jnp.float32),
            ),
            in_specs=[spec(pltpu.SMEM)] + [spec()] * 8,
            out_specs=(spec(),) * 2,
            name="look",
        )(
            brightness,
            *on_chip(near),
            *table,
            *[a.reshape(ROWS, LANES) for a in (obs_cell, obs_subhour, obs_orient, obs_value)],
        )
        whole_y = Y_BLOCKS * (columns * cell_y // Y_BLOCKS + PAD)
        line = count_x * ROWS * columns
        increment, departure = pl.pallas_call(
            main_kernel(count_x, columns, cell_y),
            out_shape=(array(ROWS, LANES), array(ROWS, LANES)),
            in_specs=[spec()] * 5,
            out_specs=(spec(), spec()),
            scratch_shapes=[pltpu.VMEM((2, rows_in_all, LANES), jnp.float32)]
            + [pltpu.VMEM((line, LANES), jnp.float32)] * 2
            + [pltpu.VMEM((whole_y, LANES), jnp.float32)] * 3,
            name="main",
        )(*on_chip(near, far, fields, indices, partial))
        return increment, departure.reshape(obs_value.shape)

    in_specs = (
        P("gx", "gy"),
        P("gx", "gy"),
        P(None, "gx", "gy"),
        P(),
        P(None, "gx"),
        P("gx", None),
        P(),
        P(),
        P("gx", "gy", None),
        P("gx", "gy", None),
        P("gx", "gy", None),
        P("gx", "gy", None),
    )
    out_specs = (P("gx", "gy"), P("gx", "gy", None))
    return jax.shard_map(
        on_device, mesh=mesh, in_specs=in_specs, out_specs=out_specs, check_vma=False
    )
```

```python
import jax
import jax.numpy as jnp
from jax import lax
from jax.experimental import pallas as pl
from jax.experimental.pallas import tpu as pltpu
from jax.sharding import PartitionSpec as P

LANES = 128
ROWS = 8
TILES = 3
Y_SETS = 2
PAD = 8


def iota(axis):
    return lax.broadcasted_iota(jnp.int32, (ROWS, LANES), axis)


def log2(size):
    assert size & (size - 1) == 0
    return size.bit_length() - 1


def spread_row(row):
    return jnp.broadcast_to(row, (ROWS, LANES))


def split(wide, pieces):
    for part in range(pieces.shape[0]):
        pieces[part] = wide[:, part * LANES : (part + 1) * LANES]


def factor_tile(first_hour, parts, bright, ratios, isotropic, horizon):
    hours = ROWS // parts
    row = iota(0)
    near_sun = jnp.zeros((ROWS, LANES), jnp.float32)
    near_edge = near_sun
    sky = near_sun
    sine = near_sun
    sun = near_sun
    for part in range(parts):
        here = row >= part * hours
        sky = jnp.where(here, spread_row(isotropic[part : part + 1, :]), sky)
        sine = jnp.where(here, spread_row(horizon[part : part + 1, :]), sine)
        for hour in range(hours):
            at = first_hour + hour
            this = row == part * hours + hour
            near_sun = jnp.where(this, bright[0, at], near_sun)
            near_edge = jnp.where(this, bright[1, at], near_edge)
            ratio = ratios[part, pl.ds(at, 1), :]
            sun = jnp.where(this, spread_row(ratio), sun)
    return (1.0 - near_sun) * sky + near_sun * sun + near_edge * sine


def pack_kernel(chips, halves, parts):
    def body(bright, table, control, std, classes, circumsolar, isotropic, horizon, payload, fields, rates, ratios):
        place_x = lax.axis_index("gx")
        place_y = lax.axis_index("gy")
        kinds, entries = table.shape
        rates[0:kinds, 0:entries] = table[...]
        rate = [
            jnp.take_along_axis(rates[pl.ds(which, ROWS, stride=0), :], classes[which], axis=1)
            for which in range(2)
        ]
        fields[0] = control[...]
        fields[1] = std[...]
        spread = control[...] * std[...] * lax.rsqrt(rate[0])
        split(circumsolar, ratios)
        mine = factor_tile(place_y * (ROWS // parts), parts, bright, ratios, isotropic, horizon)

        half = ROWS // 2
        blocks = [
            [
                jnp.concatenate([spread[:half], rate[0][:half]], 0),
                jnp.concatenate([third[:half], spread[half:]], 0),
                jnp.concatenate([rate[0][half:], third[half:]], 0),
            ]
            for third in (mine, rate[1])
        ]

        def put(chip, tiles):
            at = pl.multiple_of(chip * TILES * ROWS, ROWS)
            for tile in range(TILES):
                payload[pl.ds(at + tile * ROWS, ROWS), :] = tiles[tile]

        def fill(chip, carry):
            put(chip, blocks[0])
            return carry

        lax.fori_loop(0, chips, fill, 0, unroll=chips if chips <= 16 else 1)
        for chip in range(halves):
            put(place_x * halves + chip, blocks[1])

    return body


def look_rows(tiles, sources, keys, lane, factors):
    height = ROWS // 2

    def scan(source, factors):
        for row in range(height):
            values = tiles[pl.ds((source * TILES + 2) * height + row, ROWS, stride=0), :]
            picked = jnp.take_along_axis(values, lane, axis=1)
            factors = jnp.where(keys == source * height + row, picked, factors)
        return factors

    return lax.fori_loop(0, sources, scan, factors, unroll=sources if sources <= 32 else 1)


def look_kernel(sources, hours):
    def body(
        bright, near, circumsolar, isotropic, horizon, obs_cell, obs_subhour, obs_orient, obs_value,
        indices, partial,
    ):
        place_x = lax.axis_index("gx")
        core = lax.axis_index("gy") % 2
        hour = obs_subhour[...]
        orient = obs_orient[...]
        lane = orient & (LANES - 1)
        part_of = orient >> log2(LANES)
        home = hour - place_x * hours
        at_home = (home >= 0) & (home < hours)
        nothing = jnp.zeros((ROWS, LANES), jnp.float32)
        factors = look_rows(near, sources, jnp.where(part_of == core, hour, -1), lane, nothing)
        row = iota(0)
        for first in range(0, hours, ROWS):
            sun = nothing
            edge = nothing
            for step in range(ROWS):
                sun = jnp.where(row == step, bright[0, first + step], sun)
                edge = jnp.where(row == step, bright[1, first + step], edge)
            for part in range(2):
                ratio = circumsolar[first : first + ROWS, part * LANES : (part + 1) * LANES]
                tile = (
                    (1.0 - sun) * spread_row(isotropic[part : part + 1, :])
                    + sun * ratio
                    + edge * spread_row(horizon[part : part + 1, :])
                )
                keys = jnp.where(part_of == part, home - first, -1)
                for step in range(ROWS):
                    picked = jnp.take_along_axis(spread_row(tile[step : step + 1, :]), lane, axis=1)
                    factors = jnp.where(keys == step, picked, factors)
        indices[0] = jnp.where((part_of == core) | at_home, -1, hour)
        indices[1] = lane
        indices[2] = obs_cell[...]
        partial[0] = factors
        partial[1] = obs_value[...]

    return body


def advance(states, keep, rate, source):
    states = list(states)
    for section in range(4):
        states[section] = keep * states[section] + rate * source
        source = states[section]
    return tuple(states)


def combine(response, state):
    result = []
    for section in range(4):
        total = response[section] * state[0]
        for lower in range(1, section + 1):
            total = total + response[section - lower] * state[lower]
        result.append(total)
    return result


def main_kernel(count_x, columns, cell_y):
    steps = columns * cell_y // (Y_SETS * ROWS)
    pieces = Y_SETS * ROWS // columns
    pitch = steps + PAD
    height = ROWS // 2
    source_rows = TILES * height
    group_rows = columns * source_rows
    rows_in_all = count_x * group_rows

    def body(near, far, fields, indices, partial, increment, departure, field, ahead, smooth, source, rate, answer):
        place_x = lax.axis_index("gx")
        place_y = lax.axis_index("gy")
        core = place_y % 2
        pieces_in_all = 16 if rows_in_all > 16 * 24 else 1
        chunk = rows_in_all // pieces_in_all

        def place(at, carry):
            rows = pl.ds(pl.multiple_of(at * chunk, ROWS), chunk)
            field[core, rows, :] = near[rows, :]
            field[1 - core, rows, :] = far[rows, :]
            return carry

        lax.fori_loop(0, pieces_in_all, place, 0, unroll=pieces_in_all == 1)

        def put_column(target, column, tile):
            turned = tile.T
            for part in range(pieces):
                at = (column * pieces + part) * pitch
                target[at : at + steps, 0:ROWS] = turned[part * steps : (part + 1) * steps]

        sets = range(Y_SETS)

        def strided(step, which):
            return pl.ds(which * ROWS * pitch + step, ROWS, stride=pitch)

        rates_y = []
        for column in range(columns):
            at = column * source_rows + 2 * height
            window = pl.ds(pl.multiple_of(place_x * group_rows + at // ROWS * ROWS, ROWS), ROWS)
            inside = slice(at % ROWS, at % ROWS + height)
            tile = jnp.concatenate([field[0, window, :][inside], field[1, window, :][inside]], 0)
            rates_y.append(tile)
            put_column(rate, column, tile)

        nothing = jnp.zeros((ROWS, LANES), jnp.float32)
        block = iota(0)

        def maps_of(which):
            product = nothing + 1.0
            sums = [nothing] * 3
            for step in range(steps):
                q = rate[strided(step, which), :]
                square = q * q
                product = product * (1.0 - q)
                sums = [sums[0] + q, sums[1] + square, sums[2] + square * q]
            one, two, three = sums
            return [
                product,
                product * one,
                product * ((one * one + two) * 0.5),
                product * ((one * (one * one + 3.0 * two) + 2.0 * three) * (1.0 / 6.0)),
            ]

        def shift(values, by, fill=None):
            moved = [pltpu.roll(value, by % ROWS, 0) for value in values]
            if fill is not None:
                inside = block >= by if by > 0 else block < ROWS + by
                moved = [jnp.where(inside, value, other) for value, other in zip(moved, fill)]
            return moved

        none = [nothing] * 4
        same = [nothing + 1.0] + [nothing] * 3

        def ladders(maps):
            pairs = combine(maps, shift(maps, 1))
            fours = combine(pairs, shift(pairs, 2))
            back = [maps, shift(pairs, -1), shift(fours, -3)]
            ways = []
            for way, ladder in ((1, [maps, pairs, fours]), (-1, back)):
                total = maps
                for by in (1, 2, 4):
                    total = combine(total, shift(total, way * by, same))
                ways.append((ladder, total))
            return ways

        ladders_of = [ladders(maps_of(which)) for which in sets]

        def cells(group, row, tile):
            at = group * group_rows + tile * height + row % height
            return field[row // height, pl.ds(at, columns, stride=source_rows), :]

        still = (jnp.zeros((columns, LANES), jnp.float32),) * 4

        def forward(group, states):
            for row in range(ROWS):
                q = cells(group, row, 1)
                states = advance(states, 1.0 - q, q, cells(group, row, 0))
                ahead[pl.ds((group * ROWS + row) * columns, columns), :] = states[3]
            return states

        def backward(turn, states):
            group = count_x - 1 - turn
            for row in range(ROWS - 1, -1, -1):
                q = cells(group, row, 1)
                at = (group * ROWS + row) * columns
                states = advance(states, 1.0 - q, q, ahead[pl.ds(at, columns), :])
                smooth[pl.ds(at, columns), :] = states[3]
            return states

        unroll = count_x if count_x <= 8 else 1
        lax.fori_loop(0, count_x, forward, still, unroll=unroll)
        lax.fori_loop(0, count_x, backward, still, unroll=unroll)

        for column in range(columns):
            tile = smooth[pl.ds(place_x * ROWS * columns + column, ROWS, stride=columns), :]
            put_column(source, column, tile * lax.rsqrt(rates_y[column]))

        def line(given, result, reverse):
            order = range(steps - 1, -1, -1) if reverse else range(steps)
            way = -1 if reverse else 1

            def run(states, store):
                states = list(states)
                for step in order:
                    for which in sets:
                        at = strided(step, which)
                        q = rate[at, :]
                        states[which] = advance(states[which], 1.0 - q, q, given[at, :])
                        if store:
                            result[at, :] = states[which][3]
                return states

            leaving = run([tuple(none)] * Y_SETS, False)
            entering = [None] * Y_SETS
            before = none
            last = 0 if reverse else ROWS - 1
            locals_of = []
            for which in sets:
                ladder, total = ladders_of[which][1 if reverse else 0]
                states = leaving[which]
                for by, maps in zip((1, 2, 4), ladder):
                    added = combine(maps, shift(states, way * by, none))
                    states = [state + more for state, more in zip(states, added)]
                locals_of.append((states, total))
            for which in reversed(sets) if reverse else sets:
                states, total = locals_of[which]
                if before is not none:
                    states = [state + more for state, more in zip(states, combine(total, before))]
                entering[which] = shift(states, way, before)
                before = [spread_row(state[last : last + 1, :]) for state in states]
            run(entering, True)

        line(source, answer, False)
        line(answer, source, True)
        own = [source[pl.ds((place_y * pieces + part) * pitch, steps), :] for part in range(pieces)]
        smooth_y = jnp.concatenate(own, 0).T[0:ROWS]
        change = fields[1] * (fields[0] + smooth_y)
        increment[...] = change

        factors = look_rows(far, count_x * columns, indices[0], indices[1], partial[0])
        cell = indices[2]
        cell_lane = cell & (LANES - 1)
        cell_row = cell >> log2(LANES)
        values = nothing
        for row in range(ROWS):
            picked = jnp.take_along_axis(spread_row(change[row : row + 1, :]), cell_lane, axis=1)
            values = jnp.where(cell_row == row, picked, values)
        departure[...] = partial[1] - factors * values

    return body


def spec(space=pltpu.VMEM):
    return pl.BlockSpec(memory_space=space)


def array(*shape):
    return jax.ShapeDtypeStruct(shape, jnp.float32)


def on_chip(*arrays):
    return [pltpu.with_memory_space_constraint(a, pltpu.VMEM) for a in arrays]


def solution(mesh):
    count_x = mesh.shape["gx"]
    columns = mesh.shape["gy"]
    halves = columns // 2
    sources = count_x * columns
    rows_in_all = sources * TILES * ROWS // 2
    swap = [(place, place ^ 1) for place in range(columns)]

    def on_device(
        control,
        background_std,
        class_index,
        rate_table,
        brightness,
        circumsolar,
        isotropic,
        horizon,
        obs_cell,
        obs_subhour,
        obs_orient,
        obs_value,
    ):
        cell_x, cell_y = control.shape
        hours, orients = circumsolar.shape
        parts = orients // LANES
        assert (cell_x, cell_y) == (ROWS, LANES) and parts == 2 and hours * parts == ROWS * columns
        assert obs_value.size == ROWS * LANES
        table = (circumsolar, isotropic.reshape(parts, LANES), horizon.reshape(parts, LANES))
        payload, fields = pl.pallas_call(
            pack_kernel(count_x * halves, halves, parts),
            out_shape=(
                pltpu.VMEM((rows_in_all, LANES), jnp.float32),
                pltpu.VMEM((2, ROWS, LANES), jnp.float32),
            ),
            in_specs=[spec(pltpu.SMEM)] + [spec()] * 7,
            out_specs=(spec(),) * 2,
            scratch_shapes=[pltpu.VMEM((ROWS, LANES), jnp.float32), pltpu.VMEM((parts, hours, LANES), jnp.float32)],
            name="pack",
        )(brightness, rate_table, control, background_std, class_index, *table)
        near = lax.all_to_all(
            payload.reshape(sources, TILES, ROWS // 2, LANES), ("gx", "gy"), 0, 0, tiled=True
        ).reshape(rows_in_all, LANES)
        far = lax.ppermute(near, "gy", swap)
        indices, partial = pl.pallas_call(
            look_kernel(sources, hours),
            out_shape=(
                pltpu.VMEM((3, ROWS, LANES), jnp.int32),
                pltpu.VMEM((2, ROWS, LANES), jnp.float32),
            ),
            in_specs=[spec(pltpu.SMEM)] + [spec()] * 8,
            out_specs=(spec(),) * 2,
            name="look",
        )(
            brightness,
            *on_chip(near),
            *table,
            *[a.reshape(ROWS, LANES) for a in (obs_cell, obs_subhour, obs_orient, obs_value)],
        )
        whole_y = columns * cell_y + Y_SETS * ROWS * PAD
        line = count_x * ROWS * columns
        increment, departure = pl.pallas_call(
            main_kernel(count_x, columns, cell_y),
            out_shape=(array(ROWS, LANES), array(ROWS, LANES)),
            in_specs=[spec()] * 5,
            out_specs=(spec(), spec()),
            scratch_shapes=[pltpu.VMEM((2, rows_in_all, LANES), jnp.float32)]
            + [pltpu.VMEM((line, LANES), jnp.float32)] * 2
            + [pltpu.VMEM((whole_y, LANES), jnp.float32)] * 3,
            name="main",
        )(*on_chip(near, far, fields, indices, partial))
        return increment, departure.reshape(obs_value.shape)

    in_specs = (
        P("gx", "gy"),
        P("gx", "gy"),
        P(None, "gx", "gy"),
        P(),
        P(None, "gx"),
        P("gx", None),
        P(),
        P(),
        P("gx", "gy", None),
        P("gx", "gy", None),
        P("gx", "gy", None),
        P("gx", "gy", None),
    )
    out_specs = (P("gx", "gy"), P("gx", "gy", None))
    return jax.shard_map(
        on_device, mesh=mesh, in_specs=in_specs, out_specs=out_specs, check_vma=False
    )
```

```python
import jax
import jax.numpy as jnp
from jax import lax
from jax.experimental import pallas as pl
from jax.experimental.pallas import tpu as pltpu
from jax.sharding import PartitionSpec as P

LANES = 128
ROWS = 8
TILES = 3
Y_SETS = 2
PAD = 8


def iota(axis):
    return lax.broadcasted_iota(jnp.int32, (ROWS, LANES), axis)


def log2(size):
    assert size & (size - 1) == 0
    return size.bit_length() - 1


def loop(count, body, carry, limit=32):
    if count <= limit:
        for at in range(count):
            carry = body(at, carry)
        return carry
    return lax.fori_loop(0, count, body, carry)


def spread_row(row):
    return jnp.broadcast_to(row, (ROWS, LANES))


def split(wide, pieces):
    for part in range(pieces.shape[0]):
        pieces[part] = wide[:, part * LANES : (part + 1) * LANES]


def factor_tile(first_hour, parts, bright, ratios, isotropic, horizon):
    hours = ROWS // parts
    row = iota(0)
    near_sun = jnp.zeros((ROWS, LANES), jnp.float32)
    near_edge = near_sun
    sky = near_sun
    sine = near_sun
    sun = near_sun
    for part in range(parts):
        here = row >= part * hours
        sky = jnp.where(here, spread_row(isotropic[part : part + 1, :]), sky)
        sine = jnp.where(here, spread_row(horizon[part : part + 1, :]), sine)
        for hour in range(hours):
            at = first_hour + hour
            this = row == part * hours + hour
            near_sun = jnp.where(this, bright[0, at], near_sun)
            near_edge = jnp.where(this, bright[1, at], near_edge)
            ratio = ratios[part, pl.ds(at, 1), :]
            sun = jnp.where(this, spread_row(ratio), sun)
    return (1.0 - near_sun) * sky + near_sun * sun + near_edge * sine


def pack_kernel(count_x, columns, parts):
    def body(bright, table, control, std, classes, circumsolar, isotropic, horizon, payload, fields, rates, ratios):
        place_x = lax.axis_index("gx")
        place_y = lax.axis_index("gy")
        kinds, entries = table.shape
        rates[0:kinds, 0:entries] = table[...]
        rate = [
            jnp.take_along_axis(rates[pl.ds(which, ROWS, stride=0), :], classes[which], axis=1)
            for which in range(2)
        ]
        fields[0] = control[...]
        fields[1] = std[...]
        spread = control[...] * std[...] * lax.rsqrt(rate[0])
        split(circumsolar, ratios)
        mine = factor_tile(place_y * (ROWS // parts), parts, bright, ratios, isotropic, horizon)

        pairs = count_x // 2

        def put(pair, half, first, second):
            at = pl.multiple_of(pair * TILES * ROWS, ROWS)
            rows = slice(half * ROWS // 2, (half + 1) * ROWS // 2)
            payload[pl.ds(at, ROWS), :] = jnp.concatenate([spread[rows], rate[0][rows]], 0)
            payload[pl.ds(at + ROWS, ROWS), :] = jnp.concatenate([first[rows], spread[rows]], 0)
            payload[pl.ds(at + 2 * ROWS, ROWS), :] = jnp.concatenate([rate[0][rows], second[rows]], 0)

        even = place_x % 2 == 0
        first = jnp.where(even, rate[1], mine)
        second = jnp.where(even, mine, rate[1])
        for column in range(columns):

            def fill(pair, carry):
                put(column * pairs + pair, column % 2, mine, mine)
                return carry

            loop(pairs, fill, 0)
            put(column * pairs + place_x // 2, column % 2, first, second)

    return body


def look_rows(tiles, count_x, columns, keys, lane, factors):
    height = ROWS // 2

    def scan(source, factors):
        first = source % count_x * (columns * height) + source // count_x * height
        for row in range(height):
            values = tiles[pl.ds((source * TILES + 2) * height + row, ROWS, stride=0), :]
            picked = jnp.take_along_axis(values, lane, axis=1)
            factors = jnp.where(keys == first + row, picked, factors)
        return factors

    return loop(count_x * columns, scan, factors)


def look_kernel(count_x, columns, hours):
    def body(
        bright, near, circumsolar, isotropic, horizon, obs_cell, obs_subhour, obs_orient, obs_value,
        indices, partial,
    ):
        place_x = lax.axis_index("gx")
        core = lax.axis_index("gy") % 2
        hour = obs_subhour[...]
        orient = obs_orient[...]
        lane = orient & (LANES - 1)
        part_of = orient >> log2(LANES)
        home = hour - place_x * hours
        at_home = (home >= 0) & (home < hours)
        nothing = jnp.zeros((ROWS, LANES), jnp.float32)
        factors = look_rows(near, count_x, columns, jnp.where(part_of == core, hour, -1), lane, nothing)
        row = iota(0)
        for first in range(0, hours, ROWS):
            sun = nothing
            edge = nothing
            for step in range(ROWS):
                sun = jnp.where(row == step, bright[0, first + step], sun)
                edge = jnp.where(row == step, bright[1, first + step], edge)
            for part in range(2):
                ratio = circumsolar[first : first + ROWS, part * LANES : (part + 1) * LANES]
                tile = (
                    (1.0 - sun) * spread_row(isotropic[part : part + 1, :])
                    + sun * ratio
                    + edge * spread_row(horizon[part : part + 1, :])
                )
                keys = jnp.where(part_of == part, home - first, -1)
                for step in range(ROWS):
                    picked = jnp.take_along_axis(spread_row(tile[step : step + 1, :]), lane, axis=1)
                    factors = jnp.where(keys == step, picked, factors)
        indices[0] = jnp.where((part_of == core) | at_home, -1, hour)
        indices[1] = lane
        indices[2] = obs_cell[...]
        partial[0] = factors
        partial[1] = obs_value[...]

    return body


def advance(states, keep, rate, source):
    states = list(states)
    for section in range(4):
        states[section] = keep * states[section] + rate * source
        source = states[section]
    return tuple(states)


def combine(response, state):
    result = []
    for section in range(4):
        total = response[section] * state[0]
        for lower in range(1, section + 1):
            total = total + response[section - lower] * state[lower]
        result.append(total)
    return result


def main_kernel(count_x, columns, cell_y):
    steps = columns * cell_y // (Y_SETS * ROWS)
    pieces = Y_SETS * ROWS // columns
    pitch = steps + PAD
    height = ROWS // 2
    source_rows = TILES * height
    column_rows = count_x * source_rows
    column_pitch = column_rows + PAD

    def body(near, far, fields, indices, partial, increment, departure, field, ahead, smooth, source, rate, answer):
        place_x = lax.axis_index("gx")
        place_y = lax.axis_index("gy")
        core = place_y % 2
        for column in range(columns):
            taken = slice(column * column_rows, (column + 1) * column_rows)
            kept = slice(column * column_pitch, column * column_pitch + column_rows)
            field[core, kept, :] = near[taken, :]
            field[1 - core, kept, :] = far[taken, :]

        def cells(group, row, tile):
            at = group * source_rows + tile * height + row % height
            return field[row // height, pl.ds(at, columns, stride=column_pitch), :]

        def put_column(target, column, tile):
            turned = tile.T
            for part in range(pieces):
                at = (column * pieces + part) * pitch
                target[at : at + steps, 0:ROWS] = turned[part * steps : (part + 1) * steps]

        sets = range(Y_SETS)

        def strided(step, which):
            return pl.ds(which * ROWS * pitch + step, ROWS, stride=pitch)

        for row in range(ROWS):
            ahead[row * columns : (row + 1) * columns, :] = cells(place_x, row, 2)
        rates_y = [ahead[pl.ds(column, ROWS, stride=columns), :] for column in range(columns)]
        for column in range(columns):
            put_column(rate, column, rates_y[column])

        nothing = jnp.zeros((ROWS, LANES), jnp.float32)
        block = iota(0)

        def maps_of(which):
            product = nothing + 1.0
            sums = [nothing] * 3
            for step in range(steps):
                q = rate[strided(step, which), :]
                square = q * q
                product = product * (1.0 - q)
                sums = [sums[0] + q, sums[1] + square, sums[2] + square * q]
            one, two, three = sums
            return [
                product,
                product * one,
                product * ((one * one + two) * 0.5),
                product * ((one * (one * one + 3.0 * two) + 2.0 * three) * (1.0 / 6.0)),
            ]

        def shift(values, by, fill=None):
            moved = [pltpu.roll(value, by % ROWS, 0) for value in values]
            if fill is not None:
                inside = block >= by if by > 0 else block < ROWS + by
                moved = [jnp.where(inside, value, other) for value, other in zip(moved, fill)]
            return moved

        none = [nothing] * 4
        same = [nothing + 1.0] + [nothing] * 3

        def ladders(maps):
            pairs = combine(maps, shift(maps, 1))
            fours = combine(pairs, shift(pairs, 2))
            back = [maps, shift(pairs, -1), shift(fours, -3)]
            ways = []
            for way, ladder in ((1, [maps, pairs, fours]), (-1, back)):
                total = maps
                for by in (1, 2, 4):
                    total = combine(total, shift(total, way * by, same))
                ways.append((ladder, total))
            return ways

        ladders_of = [ladders(maps_of(which)) for which in sets]

        still = (jnp.zeros((columns, LANES), jnp.float32),) * 4

        def forward(group, states):
            for row in range(ROWS):
                q = cells(group, row, 1)
                states = advance(states, 1.0 - q, q, cells(group, row, 0))
                ahead[pl.ds((group * ROWS + row) * columns, columns), :] = states[3]
            return states

        def backward(turn, states):
            group = count_x - 1 - turn
            for row in range(ROWS - 1, -1, -1):
                q = cells(group, row, 1)
                at = (group * ROWS + row) * columns
                states = advance(states, 1.0 - q, q, ahead[pl.ds(at, columns), :])
                smooth[pl.ds(at, columns), :] = states[3]
            return states

        unroll = count_x if count_x <= 8 else 1
        lax.fori_loop(0, count_x, forward, still, unroll=unroll)
        lax.fori_loop(0, count_x, backward, still, unroll=unroll)

        for column in range(columns):
            tile = smooth[pl.ds(place_x * ROWS * columns + column, ROWS, stride=columns), :]
            put_column(source, column, tile * lax.rsqrt(rates_y[column]))

        def line(given, result, reverse):
            order = range(steps - 1, -1, -1) if reverse else range(steps)
            way = -1 if reverse else 1

            def run(states, store):
                states = list(states)
                for step in order:
                    for which in sets:
                        at = strided(step, which)
                        q = rate[at, :]
                        states[which] = advance(states[which], 1.0 - q, q, given[at, :])
                        if store:
                            result[at, :] = states[which][3]
                return states

            leaving = run([tuple(none)] * Y_SETS, False)
            entering = [None] * Y_SETS
            before = none
            last = 0 if reverse else ROWS - 1
            locals_of = []
            for which in sets:
                ladder, total = ladders_of[which][1 if reverse else 0]
                states = leaving[which]
                for by, maps in zip((1, 2, 4), ladder):
                    added = combine(maps, shift(states, way * by, none))
                    states = [state + more for state, more in zip(states, added)]
                locals_of.append((states, total))
            for which in reversed(sets) if reverse else sets:
                states, total = locals_of[which]
                if before is not none:
                    states = [state + more for state, more in zip(states, combine(total, before))]
                entering[which] = shift(states, way, before)
                before = [spread_row(state[last : last + 1, :]) for state in states]
            run(entering, True)

        line(source, answer, False)
        line(answer, source, True)
        own = [source[pl.ds((place_y * pieces + part) * pitch, steps), :] for part in range(pieces)]
        smooth_y = jnp.concatenate(own, 0).T[0:ROWS]
        change = fields[1] * (fields[0] + smooth_y)
        increment[...] = change

        factors = look_rows(far, count_x, columns, indices[0], indices[1], partial[0])
        cell = indices[2]
        cell_lane = cell & (LANES - 1)
        cell_row = cell >> log2(LANES)
        values = nothing
        for row in range(ROWS):
            picked = jnp.take_along_axis(spread_row(change[row : row + 1, :]), cell_lane, axis=1)
            values = jnp.where(cell_row == row, picked, values)
        departure[...] = partial[1] - factors * values

    return body


def spec(space=pltpu.VMEM):
    return pl.BlockSpec(memory_space=space)


def array(*shape):
    return jax.ShapeDtypeStruct(shape, jnp.float32)


def on_chip(*arrays):
    return [pltpu.with_memory_space_constraint(a, pltpu.VMEM) for a in arrays]


def solution(mesh):
    count_x = mesh.shape["gx"]
    columns = mesh.shape["gy"]
    sources = count_x * columns
    rows_in_all = sources * TILES * ROWS // 2
    swap = [(place, place ^ 1) for place in range(columns)]

    def on_device(
        control,
        background_std,
        class_index,
        rate_table,
        brightness,
        circumsolar,
        isotropic,
        horizon,
        obs_cell,
        obs_subhour,
        obs_orient,
        obs_value,
    ):
        cell_x, cell_y = control.shape
        hours, orients = circumsolar.shape
        parts = orients // LANES
        assert (cell_x, cell_y) == (ROWS, LANES) and parts == 2 and hours * parts == ROWS * columns
        assert obs_value.size == ROWS * LANES
        table = (circumsolar, isotropic.reshape(parts, LANES), horizon.reshape(parts, LANES))
        payload, fields = pl.pallas_call(
            pack_kernel(count_x, columns, parts),
            out_shape=(
                pltpu.VMEM((rows_in_all, LANES), jnp.float32),
                pltpu.VMEM((2, ROWS, LANES), jnp.float32),
            ),
            in_specs=[spec(pltpu.SMEM)] + [spec()] * 7,
            out_specs=(spec(),) * 2,
            scratch_shapes=[pltpu.VMEM((ROWS, LANES), jnp.float32), pltpu.VMEM((parts, hours, LANES), jnp.float32)],
            name="pack",
        )(brightness, rate_table, control, background_std, class_index, *table)
        near = lax.all_to_all(
            payload.reshape(sources, TILES, ROWS // 2, LANES), ("gy", "gx"), 0, 0, tiled=True
        ).reshape(rows_in_all, LANES)
        far = lax.ppermute(near, "gy", swap)
        indices, partial = pl.pallas_call(
            look_kernel(count_x, columns, hours),
            out_shape=(
                pltpu.VMEM((3, ROWS, LANES), jnp.int32),
                pltpu.VMEM((2, ROWS, LANES), jnp.float32),
            ),
            in_specs=[spec(pltpu.SMEM)] + [spec()] * 8,
            out_specs=(spec(),) * 2,
            name="look",
        )(
            brightness,
            *on_chip(near),
            *table,
            *[a.reshape(ROWS, LANES) for a in (obs_cell, obs_subhour, obs_orient, obs_value)],
        )
        whole_y = columns * cell_y + Y_SETS * ROWS * PAD
        line = count_x * ROWS * columns
        increment, departure = pl.pallas_call(
            main_kernel(count_x, columns, cell_y),
            out_shape=(array(ROWS, LANES), array(ROWS, LANES)),
            in_specs=[spec()] * 5,
            out_specs=(spec(), spec()),
            scratch_shapes=[pltpu.VMEM((2, rows_in_all + columns * PAD, LANES), jnp.float32)]
            + [pltpu.VMEM((line, LANES), jnp.float32)] * 2
            + [pltpu.VMEM((whole_y, LANES), jnp.float32)] * 3,
            name="main",
        )(*on_chip(near, far, fields, indices, partial))
        return increment, departure.reshape(obs_value.shape)

    in_specs = (
        P("gx", "gy"),
        P("gx", "gy"),
        P(None, "gx", "gy"),
        P(),
        P(None, "gx"),
        P("gx", None),
        P(),
        P(),
        P("gx", "gy", None),
        P("gx", "gy", None),
        P("gx", "gy", None),
        P("gx", "gy", None),
    )
    out_specs = (P("gx", "gy"), P("gx", "gy", None))
    return jax.shard_map(
        on_device, mesh=mesh, in_specs=in_specs, out_specs=out_specs, check_vma=False
    )
```

```python
import jax
import jax.numpy as jnp
from jax import lax
from jax.experimental import pallas as pl
from jax.experimental.pallas import tpu as pltpu
from jax.sharding import PartitionSpec as P

LANES = 128
ROWS = 8
TILES = 3
Y_SETS = 2
PAD = 8


def iota(axis):
    return lax.broadcasted_iota(jnp.int32, (ROWS, LANES), axis)


def log2(size):
    assert size & (size - 1) == 0
    return size.bit_length() - 1


def loop(count, body, carry, limit=32):
    if count <= limit:
        for at in range(count):
            carry = body(at, carry)
        return carry
    return lax.fori_loop(0, count, body, carry)


def slot(place, count):
    flip = 0
    for bit in range(1, log2(count)):
        flip = flip ^ (place >> bit & 1)
    return place ^ flip


def spread_row(row):
    return jnp.broadcast_to(row, (ROWS, LANES))


def split(wide, pieces):
    for part in range(pieces.shape[0]):
        pieces[part] = wide[:, part * LANES : (part + 1) * LANES]


def factor_tile(first_hour, parts, bright, ratios, isotropic, horizon):
    hours = ROWS // parts
    row = iota(0)
    near_sun = jnp.zeros((ROWS, LANES), jnp.float32)
    near_edge = near_sun
    sky = near_sun
    sine = near_sun
    sun = near_sun
    for part in range(parts):
        here = row >= part * hours
        sky = jnp.where(here, spread_row(isotropic[part : part + 1, :]), sky)
        sine = jnp.where(here, spread_row(horizon[part : part + 1, :]), sine)
        for hour in range(hours):
            at = first_hour + hour
            this = row == part * hours + hour
            near_sun = jnp.where(this, bright[0, at], near_sun)
            near_edge = jnp.where(this, bright[1, at], near_edge)
            ratio = ratios[part, pl.ds(at, 1), :]
            sun = jnp.where(this, spread_row(ratio), sun)
    return (1.0 - near_sun) * sky + near_sun * sun + near_edge * sine


def pack_kernel(count_x, columns, parts):
    def body(bright, table, control, std, classes, circumsolar, isotropic, horizon, payload, fields, rates, ratios):
        place_x = lax.axis_index("gx")
        place_y = lax.axis_index("gy")
        kinds, entries = table.shape
        rates[0:kinds, 0:entries] = table[...]
        rate = [
            jnp.take_along_axis(rates[pl.ds(which, ROWS, stride=0), :], classes[which], axis=1)
            for which in range(2)
        ]
        fields[0] = control[...]
        fields[1] = std[...]
        spread = control[...] * std[...] * lax.rsqrt(rate[0])
        split(circumsolar, ratios)
        mine = factor_tile(place_y * (ROWS // parts), parts, bright, ratios, isotropic, horizon)

        pairs = count_x // 2

        def put(pair, half, first, second):
            at = pl.multiple_of(pair * TILES * ROWS, ROWS)
            rows = slice(half * ROWS // 2, (half + 1) * ROWS // 2)
            payload[pl.ds(at, ROWS), :] = jnp.concatenate([spread[rows], rate[0][rows]], 0)
            payload[pl.ds(at + ROWS, ROWS), :] = jnp.concatenate([first[rows], spread[rows]], 0)
            payload[pl.ds(at + 2 * ROWS, ROWS), :] = jnp.concatenate([rate[0][rows], second[rows]], 0)

        even = slot(place_x, count_x) % 2 == 0
        first = jnp.where(even, rate[1], mine)
        second = jnp.where(even, mine, rate[1])
        for column in range(columns):

            def fill(pair, carry):
                put(column * pairs + pair, column % 2, mine, mine)
                return carry

            loop(pairs, fill, 0)
            put(column * pairs + place_x // 2, column % 2, first, second)

    return body


def look_rows(tiles, count_x, columns, keys, lane, factors):
    height = ROWS // 2

    def scan(source, factors):
        first = slot(source % count_x, count_x) * (columns * height) + source // count_x * height
        for row in range(height):
            values = tiles[pl.ds((source * TILES + 2) * height + row, ROWS, stride=0), :]
            picked = jnp.take_along_axis(values, lane, axis=1)
            factors = jnp.where(keys == first + row, picked, factors)
        return factors

    return loop(count_x * columns, scan, factors)


def look_kernel(count_x, columns, hours):
    def body(
        bright, near, circumsolar, isotropic, horizon, obs_cell, obs_subhour, obs_orient, obs_value,
        indices, partial,
    ):
        place_x = lax.axis_index("gx")
        core = lax.axis_index("gy") % 2
        hour = obs_subhour[...]
        orient = obs_orient[...]
        lane = orient & (LANES - 1)
        part_of = orient >> log2(LANES)
        home = hour - place_x * hours
        at_home = (home >= 0) & (home < hours)
        nothing = jnp.zeros((ROWS, LANES), jnp.float32)
        factors = look_rows(near, count_x, columns, jnp.where(part_of == core, hour, -1), lane, nothing)
        row = iota(0)
        for first in range(0, hours, ROWS):
            sun = nothing
            edge = nothing
            for step in range(ROWS):
                sun = jnp.where(row == step, bright[0, first + step], sun)
                edge = jnp.where(row == step, bright[1, first + step], edge)
            for part in range(2):
                ratio = circumsolar[first : first + ROWS, part * LANES : (part + 1) * LANES]
                tile = (
                    (1.0 - sun) * spread_row(isotropic[part : part + 1, :])
                    + sun * ratio
                    + edge * spread_row(horizon[part : part + 1, :])
                )
                keys = jnp.where(part_of == part, home - first, -1)
                for step in range(ROWS):
                    picked = jnp.take_along_axis(spread_row(tile[step : step + 1, :]), lane, axis=1)
                    factors = jnp.where(keys == step, picked, factors)
        indices[0] = jnp.where((part_of == core) | at_home, -1, hour)
        indices[1] = lane
        indices[2] = obs_cell[...]
        partial[0] = factors
        partial[1] = obs_value[...]

    return body


def advance(states, keep, rate, source):
    states = list(states)
    for section in range(4):
        states[section] = keep * states[section] + rate * source
        source = states[section]
    return tuple(states)


def combine(response, state):
    result = []
    for section in range(4):
        total = response[section] * state[0]
        for lower in range(1, section + 1):
            total = total + response[section - lower] * state[lower]
        result.append(total)
    return result


def main_kernel(count_x, columns, cell_y):
    steps = columns * cell_y // (Y_SETS * ROWS)
    pieces = Y_SETS * ROWS // columns
    pitch = steps + PAD
    height = ROWS // 2
    source_rows = TILES * height
    column_rows = count_x * source_rows
    column_pitch = column_rows + PAD

    def body(near, far, fields, indices, partial, increment, departure, field, ahead, smooth, source, rate, answer):
        place_x = lax.axis_index("gx")
        place_y = lax.axis_index("gy")
        core = place_y % 2
        for column in range(columns):
            taken = slice(column * column_rows, (column + 1) * column_rows)
            kept = slice(column * column_pitch, column * column_pitch + column_rows)
            field[core, kept, :] = near[taken, :]
            field[1 - core, kept, :] = far[taken, :]

        def cells(group, row, tile):
            at = slot(group, count_x) * source_rows + tile * height + row % height
            return field[row // height, pl.ds(at, columns, stride=column_pitch), :]

        def put_column(target, column, tile):
            turned = tile.T
            for part in range(pieces):
                at = (column * pieces + part) * pitch
                target[at : at + steps, 0:ROWS] = turned[part * steps : (part + 1) * steps]

        sets = range(Y_SETS)

        def strided(step, which):
            return pl.ds(which * ROWS * pitch + step, ROWS, stride=pitch)

        for row in range(ROWS):
            ahead[row * columns : (row + 1) * columns, :] = cells(place_x, row, 2)
        rates_y = [ahead[pl.ds(column, ROWS, stride=columns), :] for column in range(columns)]
        for column in range(columns):
            put_column(rate, column, rates_y[column])

        nothing = jnp.zeros((ROWS, LANES), jnp.float32)
        block = iota(0)

        def maps_of(which):
            product = nothing + 1.0
            sums = [nothing] * 3
            for step in range(steps):
                q = rate[strided(step, which), :]
                square = q * q
                product = product * (1.0 - q)
                sums = [sums[0] + q, sums[1] + square, sums[2] + square * q]
            one, two, three = sums
            return [
                product,
                product * one,
                product * ((one * one + two) * 0.5),
                product * ((one * (one * one + 3.0 * two) + 2.0 * three) * (1.0 / 6.0)),
            ]

        def shift(values, by, fill=None):
            moved = [pltpu.roll(value, by % ROWS, 0) for value in values]
            if fill is not None:
                inside = block >= by if by > 0 else block < ROWS + by
                moved = [jnp.where(inside, value, other) for value, other in zip(moved, fill)]
            return moved

        none = [nothing] * 4
        same = [nothing + 1.0] + [nothing] * 3

        def ladders(maps):
            pairs = combine(maps, shift(maps, 1))
            fours = combine(pairs, shift(pairs, 2))
            back = [maps, shift(pairs, -1), shift(fours, -3)]
            ways = []
            for way, ladder in ((1, [maps, pairs, fours]), (-1, back)):
                total = maps
                for by in (1, 2, 4):
                    total = combine(total, shift(total, way * by, same))
                ways.append((ladder, total))
            return ways

        ladders_of = [ladders(maps_of(which)) for which in sets]

        still = (jnp.zeros((columns, LANES), jnp.float32),) * 4

        def forward(group, states):
            for row in range(ROWS):
                q = cells(group, row, 1)
                states = advance(states, 1.0 - q, q, cells(group, row, 0))
                ahead[pl.ds((group * ROWS + row) * columns, columns), :] = states[3]
            return states

        def backward(turn, states):
            group = count_x - 1 - turn
            for row in range(ROWS - 1, -1, -1):
                q = cells(group, row, 1)
                at = (group * ROWS + row) * columns
                states = advance(states, 1.0 - q, q, ahead[pl.ds(at, columns), :])
                smooth[pl.ds(at, columns), :] = states[3]
            return states

        unroll = count_x if count_x <= 8 else 1
        lax.fori_loop(0, count_x, forward, still, unroll=unroll)
        lax.fori_loop(0, count_x, backward, still, unroll=unroll)

        for column in range(columns):
            tile = smooth[pl.ds(place_x * ROWS * columns + column, ROWS, stride=columns), :]
            put_column(source, column, tile * lax.rsqrt(rates_y[column]))

        def line(given, result, reverse):
            order = range(steps - 1, -1, -1) if reverse else range(steps)
            way = -1 if reverse else 1

            def run(states, store):
                states = list(states)
                for step in order:
                    for which in sets:
                        at = strided(step, which)
                        q = rate[at, :]
                        states[which] = advance(states[which], 1.0 - q, q, given[at, :])
                        if store:
                            result[at, :] = states[which][3]
                return states

            leaving = run([tuple(none)] * Y_SETS, False)
            entering = [None] * Y_SETS
            before = none
            last = 0 if reverse else ROWS - 1
            locals_of = []
            for which in sets:
                ladder, total = ladders_of[which][1 if reverse else 0]
                states = leaving[which]
                for by, maps in zip((1, 2, 4), ladder):
                    added = combine(maps, shift(states, way * by, none))
                    states = [state + more for state, more in zip(states, added)]
                locals_of.append((states, total))
            for which in reversed(sets) if reverse else sets:
                states, total = locals_of[which]
                if before is not none:
                    states = [state + more for state, more in zip(states, combine(total, before))]
                entering[which] = shift(states, way, before)
                before = [spread_row(state[last : last + 1, :]) for state in states]
            run(entering, True)

        line(source, answer, False)
        line(answer, source, True)
        own = [source[pl.ds((place_y * pieces + part) * pitch, steps), :] for part in range(pieces)]
        smooth_y = jnp.concatenate(own, 0).T[0:ROWS]
        change = fields[1] * (fields[0] + smooth_y)
        increment[...] = change

        factors = look_rows(far, count_x, columns, indices[0], indices[1], partial[0])
        cell = indices[2]
        cell_lane = cell & (LANES - 1)
        cell_row = cell >> log2(LANES)
        values = nothing
        for row in range(ROWS):
            picked = jnp.take_along_axis(spread_row(change[row : row + 1, :]), cell_lane, axis=1)
            values = jnp.where(cell_row == row, picked, values)
        departure[...] = partial[1] - factors * values

    return body


def spec(space=pltpu.VMEM):
    return pl.BlockSpec(memory_space=space)


def array(*shape):
    return jax.ShapeDtypeStruct(shape, jnp.float32)


def on_chip(*arrays):
    return [pltpu.with_memory_space_constraint(a, pltpu.VMEM) for a in arrays]


def solution(mesh):
    count_x = mesh.shape["gx"]
    columns = mesh.shape["gy"]
    sources = count_x * columns
    rows_in_all = sources * TILES * ROWS // 2
    members = [line * count_x + slot(place, count_x) for line in range(columns) for place in range(count_x)]
    swap = [(place, place ^ 1) for place in range(columns)]

    def on_device(
        control,
        background_std,
        class_index,
        rate_table,
        brightness,
        circumsolar,
        isotropic,
        horizon,
        obs_cell,
        obs_subhour,
        obs_orient,
        obs_value,
    ):
        cell_x, cell_y = control.shape
        hours, orients = circumsolar.shape
        parts = orients // LANES
        assert (cell_x, cell_y) == (ROWS, LANES) and parts == 2 and hours * parts == ROWS * columns
        assert obs_value.size == ROWS * LANES
        table = (circumsolar, isotropic.reshape(parts, LANES), horizon.reshape(parts, LANES))
        payload, fields = pl.pallas_call(
            pack_kernel(count_x, columns, parts),
            out_shape=(
                pltpu.VMEM((rows_in_all, LANES), jnp.float32),
                pltpu.VMEM((2, ROWS, LANES), jnp.float32),
            ),
            in_specs=[spec(pltpu.SMEM)] + [spec()] * 7,
            out_specs=(spec(),) * 2,
            scratch_shapes=[pltpu.VMEM((ROWS, LANES), jnp.float32), pltpu.VMEM((parts, hours, LANES), jnp.float32)],
            name="pack",
        )(brightness, rate_table, control, background_std, class_index, *table)
        near = lax.all_to_all(
            payload.reshape(sources, TILES, ROWS // 2, LANES), ("gy", "gx"), 0, 0,
            axis_index_groups=[members], tiled=True
        ).reshape(rows_in_all, LANES)
        far = lax.ppermute(near, "gy", swap)
        indices, partial = pl.pallas_call(
            look_kernel(count_x, columns, hours),
            out_shape=(
                pltpu.VMEM((3, ROWS, LANES), jnp.int32),
                pltpu.VMEM((2, ROWS, LANES), jnp.float32),
            ),
            in_specs=[spec(pltpu.SMEM)] + [spec()] * 8,
            out_specs=(spec(),) * 2,
            name="look",
        )(
            brightness,
            *on_chip(near),
            *table,
            *[a.reshape(ROWS, LANES) for a in (obs_cell, obs_subhour, obs_orient, obs_value)],
        )
        whole_y = columns * cell_y + Y_SETS * ROWS * PAD
        line = count_x * ROWS * columns
        increment, departure = pl.pallas_call(
            main_kernel(count_x, columns, cell_y),
            out_shape=(array(ROWS, LANES), array(ROWS, LANES)),
            in_specs=[spec()] * 5,
            out_specs=(spec(), spec()),
            scratch_shapes=[pltpu.VMEM((2, rows_in_all + columns * PAD, LANES), jnp.float32)]
            + [pltpu.VMEM((line, LANES), jnp.float32)] * 2
            + [pltpu.VMEM((whole_y, LANES), jnp.float32)] * 3,
            name="main",
        )(*on_chip(near, far, fields, indices, partial))
        return increment, departure.reshape(obs_value.shape)

    in_specs = (
        P("gx", "gy"),
        P("gx", "gy"),
        P(None, "gx", "gy"),
        P(),
        P(None, "gx"),
        P("gx", None),
        P(),
        P(),
        P("gx", "gy", None),
        P("gx", "gy", None),
        P("gx", "gy", None),
        P("gx", "gy", None),
    )
    out_specs = (P("gx", "gy"), P("gx", "gy", None))
    return jax.shard_map(
        on_device, mesh=mesh, in_specs=in_specs, out_specs=out_specs, check_vma=False
    )
```

```python
import jax
import jax.numpy as jnp
from jax import lax
from jax.experimental import pallas as pl
from jax.experimental.pallas import tpu as pltpu
from jax.sharding import PartitionSpec as P

LANES = 128
ROWS = 8
TILES = 3
Y_SETS = 2
PAD = 8


def iota(axis):
    return lax.broadcasted_iota(jnp.int32, (ROWS, LANES), axis)


def log2(size):
    assert size & (size - 1) == 0
    return size.bit_length() - 1


def loop(count, body, carry, limit=32):
    if count <= limit:
        for at in range(count):
            carry = body(at, carry)
        return carry
    return lax.fori_loop(0, count, body, carry)


def slot(place, count):
    flip = 0
    for bit in range(1, log2(count)):
        flip = flip ^ (place >> bit & 1)
    return place ^ flip


def spread_row(row):
    return jnp.broadcast_to(row, (ROWS, LANES))


def split(wide, pieces):
    for part in range(pieces.shape[0]):
        pieces[part] = wide[:, part * LANES : (part + 1) * LANES]


def factor_tile(first_hour, parts, bright, ratios, isotropic, horizon):
    hours = ROWS // parts
    row = iota(0)
    near_sun = jnp.zeros((ROWS, LANES), jnp.float32)
    near_edge = near_sun
    sky = near_sun
    sine = near_sun
    sun = near_sun
    for part in range(parts):
        here = row >= part * hours
        sky = jnp.where(here, spread_row(isotropic[part : part + 1, :]), sky)
        sine = jnp.where(here, spread_row(horizon[part : part + 1, :]), sine)
        for hour in range(hours):
            at = first_hour + hour
            this = row == part * hours + hour
            near_sun = jnp.where(this, bright[0, at], near_sun)
            near_edge = jnp.where(this, bright[1, at], near_edge)
            ratio = ratios[part, pl.ds(at, 1), :]
            sun = jnp.where(this, spread_row(ratio), sun)
    return (1.0 - near_sun) * sky + near_sun * sun + near_edge * sine


def pack_kernel(count_x, columns, parts):
    def body(bright, table, control, std, classes, circumsolar, isotropic, horizon, payload, fields, rates, ratios):
        place_x = lax.axis_index("gx")
        place_y = lax.axis_index("gy")
        kinds, entries = table.shape
        rates[0:kinds, 0:entries] = table[...]
        rate = [
            jnp.take_along_axis(rates[pl.ds(which, ROWS, stride=0), :], classes[which], axis=1)
            for which in range(2)
        ]
        fields[0] = control[...]
        fields[1] = std[...]
        spread = control[...] * std[...] * lax.rsqrt(rate[0])
        split(circumsolar, ratios)
        mine = factor_tile(place_y * (ROWS // parts), parts, bright, ratios, isotropic, horizon)

        pairs = count_x // 2

        def put(pair, half, first, second):
            at = pl.multiple_of(pair * TILES * ROWS, ROWS)
            rows = slice(half * ROWS // 2, (half + 1) * ROWS // 2)
            payload[pl.ds(at, ROWS), :] = jnp.concatenate([spread[rows], rate[0][rows]], 0)
            payload[pl.ds(at + ROWS, ROWS), :] = jnp.concatenate([first[rows], spread[rows]], 0)
            payload[pl.ds(at + 2 * ROWS, ROWS), :] = jnp.concatenate([rate[0][rows], second[rows]], 0)

        even = slot(place_x, count_x) % 2 == 0
        first = jnp.where(even, rate[1], mine)
        second = jnp.where(even, mine, rate[1])
        for column in range(columns):

            def fill(pair, carry):
                put(column * pairs + pair, column % 2, mine, mine)
                return carry

            loop(pairs, fill, 0)
            put(column * pairs + place_x // 2, column % 2, first, second)

    return body


def look_rows(tiles, count_x, columns, keys, lane, factors):
    height = ROWS // 2

    def scan(source, factors):
        first = slot(source % count_x, count_x) * (columns * height) + source // count_x * height
        for row in range(height):
            values = tiles[pl.ds((source * TILES + 2) * height + row, ROWS, stride=0), :]
            picked = jnp.take_along_axis(values, lane, axis=1)
            factors = jnp.where(keys == first + row, picked, factors)
        return factors

    return loop(count_x * columns, scan, factors)


def look_kernel(count_x, columns, hours):
    def body(
        bright, near, circumsolar, isotropic, horizon, obs_cell, obs_subhour, obs_orient, obs_value,
        indices, partial,
    ):
        place_x = lax.axis_index("gx")
        core = lax.axis_index("gy") % 2
        hour = obs_subhour[...]
        orient = obs_orient[...]
        lane = orient & (LANES - 1)
        part_of = orient >> log2(LANES)
        home = hour - place_x * hours
        at_home = (home >= 0) & (home < hours)
        nothing = jnp.zeros((ROWS, LANES), jnp.float32)
        factors = look_rows(near, count_x, columns, jnp.where(part_of == core, hour, -1), lane, nothing)
        row = iota(0)
        for first in range(0, hours, ROWS):
            sun = nothing
            edge = nothing
            for step in range(ROWS):
                sun = jnp.where(row == step, bright[0, first + step], sun)
                edge = jnp.where(row == step, bright[1, first + step], edge)
            for part in range(2):
                ratio = circumsolar[first : first + ROWS, part * LANES : (part + 1) * LANES]
                tile = (
                    (1.0 - sun) * spread_row(isotropic[part : part + 1, :])
                    + sun * ratio
                    + edge * spread_row(horizon[part : part + 1, :])
                )
                keys = jnp.where(part_of == part, home - first, -1)
                for step in range(ROWS):
                    picked = jnp.take_along_axis(spread_row(tile[step : step + 1, :]), lane, axis=1)
                    factors = jnp.where(keys == step, picked, factors)
        indices[0] = jnp.where((part_of == core) | at_home, -1, hour)
        indices[1] = lane
        indices[2] = obs_cell[...]
        partial[0] = factors
        partial[1] = obs_value[...]

    return body


def advance(states, keep, rate, source):
    states = list(states)
    for section in range(4):
        states[section] = keep * states[section] + rate * source
        source = states[section]
    return tuple(states)


def combine(response, state):
    result = []
    for section in range(4):
        total = response[section] * state[0]
        for lower in range(1, section + 1):
            total = total + response[section - lower] * state[lower]
        result.append(total)
    return result


def main_kernel(count_x, columns, cell_y):
    assert columns % Y_SETS == 0
    steps = columns * cell_y // (Y_SETS * ROWS)
    pieces = Y_SETS * ROWS // columns
    pitch = steps + PAD
    height = ROWS // 2
    source_rows = TILES * height
    column_rows = count_x * source_rows
    column_pitch = column_rows + PAD

    def body(near, far, fields, indices, partial, increment, departure, field, ahead, smooth, source, rate, answer):
        place_x = lax.axis_index("gx")
        place_y = lax.axis_index("gy")
        core = place_y % 2
        for column in range(columns):
            taken = slice(column * column_rows, (column + 1) * column_rows)
            kept = slice(column * column_pitch, column * column_pitch + column_rows)
            field[core, kept, :] = near[taken, :]
            field[1 - core, kept, :] = far[taken, :]

        def cells(group, row, tile):
            at = slot(group, count_x) * source_rows + tile * height + row % height
            return field[row // height, pl.ds(at, columns, stride=column_pitch), :]

        def put_column(target, column, tile):
            turned = tile.T
            for part in range(pieces):
                at = (column * pieces + part) * pitch
                target[at : at + steps, 0:ROWS] = turned[part * steps : (part + 1) * steps]

        sets = range(Y_SETS)

        def strided(step, which):
            return pl.ds(which * ROWS * pitch + step, ROWS, stride=pitch)

        for row in range(ROWS):
            ahead[row * columns : (row + 1) * columns, :] = cells(place_x, row, 2)
        rates_y = [ahead[pl.ds(column, ROWS, stride=columns), :] for column in range(columns)]
        for column in range(columns):
            put_column(rate, column, rates_y[column])

        nothing = jnp.zeros((ROWS, LANES), jnp.float32)
        block = iota(0)

        def maps_of(which):
            product = nothing + 1.0
            sums = [nothing] * 3
            for step in range(steps):
                q = rate[strided(step, which), :]
                square = q * q
                product = product * (1.0 - q)
                sums = [sums[0] + q, sums[1] + square, sums[2] + square * q]
            one, two, three = sums
            return [
                product,
                product * one,
                product * ((one * one + two) * 0.5),
                product * ((one * (one * one + 3.0 * two) + 2.0 * three) * (1.0 / 6.0)),
            ]

        def shift(values, by, fill=None):
            moved = [pltpu.roll(value, by % ROWS, 0) for value in values]
            if fill is not None:
                inside = block >= by if by > 0 else block < ROWS + by
                moved = [jnp.where(inside, value, other) for value, other in zip(moved, fill)]
            return moved

        none = [nothing] * 4
        same = [nothing + 1.0] + [nothing] * 3

        def ladders(maps):
            pairs = combine(maps, shift(maps, 1))
            fours = combine(pairs, shift(pairs, 2))
            back = [maps, shift(pairs, -1), shift(fours, -3)]
            ways = []
            for way, ladder in ((1, [maps, pairs, fours]), (-1, back)):
                total = maps
                for by in (1, 2, 4):
                    total = combine(total, shift(total, way * by, same))
                ways.append((ladder, total))
            return ways

        ladders_of = [ladders(maps_of(which)) for which in sets]

        still = (jnp.zeros((columns, LANES), jnp.float32),) * 4

        def forward(group, states):
            for row in range(ROWS):
                q = cells(group, row, 1)
                states = advance(states, 1.0 - q, q, cells(group, row, 0))
                ahead[pl.ds((group * ROWS + row) * columns, columns), :] = states[3]
            return states

        def backward(turn, states):
            group = count_x - 1 - turn
            for row in range(ROWS - 1, -1, -1):
                q = cells(group, row, 1)
                at = (group * ROWS + row) * columns
                states = advance(states, 1.0 - q, q, ahead[pl.ds(at, columns), :])
                smooth[pl.ds(at, columns), :] = states[3]
            return states

        unroll = count_x if count_x <= 8 else 1
        lax.fori_loop(0, count_x, forward, still, unroll=unroll)
        lax.fori_loop(0, count_x, backward, still, unroll=unroll)

        for column in range(columns):
            tile = smooth[pl.ds(place_x * ROWS * columns + column, ROWS, stride=columns), :]
            put_column(source, column, tile * lax.rsqrt(rates_y[column]))

        def line(given, result, reverse):
            order = range(steps - 1, -1, -1) if reverse else range(steps)
            way = -1 if reverse else 1

            def run(states, store):
                states = list(states)
                for step in order:
                    for which in sets:
                        at = strided(step, which)
                        q = rate[at, :]
                        states[which] = advance(states[which], 1.0 - q, q, given[at, :])
                        if store:
                            result[at, :] = states[which][3]
                return states

            leaving = run([tuple(none)] * Y_SETS, False)
            entering = [None] * Y_SETS
            before = none
            last = 0 if reverse else ROWS - 1
            locals_of = []
            for which in sets:
                ladder, total = ladders_of[which][1 if reverse else 0]
                states = leaving[which]
                for by, maps in zip((1, 2, 4), ladder):
                    added = combine(maps, shift(states, way * by, none))
                    states = [state + more for state, more in zip(states, added)]
                locals_of.append((states, total))
            for which in reversed(sets) if reverse else sets:
                states, total = locals_of[which]
                if before is not none:
                    states = [state + more for state, more in zip(states, combine(total, before))]
                entering[which] = shift(states, way, before)
                before = [spread_row(state[last : last + 1, :]) for state in states]
            if not reverse:
                run(entering, True)
                return
            mine = place_y // (columns // Y_SETS)
            states = entering[0]
            for which in sets[1:]:
                states = [jnp.where(mine == which, new, old) for new, old in zip(entering[which], states)]
            for step in order:
                at = strided(step, mine)
                q = rate[at, :]
                states = advance(states, 1.0 - q, q, given[at, :])
                result[at, :] = states[3]

        line(source, answer, False)
        line(answer, source, True)
        own = [source[pl.ds((place_y * pieces + part) * pitch, steps), :] for part in range(pieces)]
        smooth_y = jnp.concatenate(own, 0).T[0:ROWS]
        change = fields[1] * (fields[0] + smooth_y)
        increment[...] = change

        factors = look_rows(far, count_x, columns, indices[0], indices[1], partial[0])
        cell = indices[2]
        cell_lane = cell & (LANES - 1)
        cell_row = cell >> log2(LANES)
        values = nothing
        for row in range(ROWS):
            picked = jnp.take_along_axis(spread_row(change[row : row + 1, :]), cell_lane, axis=1)
            values = jnp.where(cell_row == row, picked, values)
        departure[...] = partial[1] - factors * values

    return body


def spec(space=pltpu.VMEM):
    return pl.BlockSpec(memory_space=space)


def array(*shape):
    return jax.ShapeDtypeStruct(shape, jnp.float32)


def on_chip(*arrays):
    return [pltpu.with_memory_space_constraint(a, pltpu.VMEM) for a in arrays]


def solution(mesh):
    count_x = mesh.shape["gx"]
    columns = mesh.shape["gy"]
    sources = count_x * columns
    rows_in_all = sources * TILES * ROWS // 2
    members = [line * count_x + slot(place, count_x) for line in range(columns) for place in range(count_x)]
    swap = [(place, place ^ 1) for place in range(columns)]

    def on_device(
        control,
        background_std,
        class_index,
        rate_table,
        brightness,
        circumsolar,
        isotropic,
        horizon,
        obs_cell,
        obs_subhour,
        obs_orient,
        obs_value,
    ):
        cell_x, cell_y = control.shape
        hours, orients = circumsolar.shape
        parts = orients // LANES
        assert (cell_x, cell_y) == (ROWS, LANES) and parts == 2 and hours * parts == ROWS * columns
        assert obs_value.size == ROWS * LANES
        table = (circumsolar, isotropic.reshape(parts, LANES), horizon.reshape(parts, LANES))
        payload, fields = pl.pallas_call(
            pack_kernel(count_x, columns, parts),
            out_shape=(
                pltpu.VMEM((rows_in_all, LANES), jnp.float32),
                pltpu.VMEM((2, ROWS, LANES), jnp.float32),
            ),
            in_specs=[spec(pltpu.SMEM)] + [spec()] * 7,
            out_specs=(spec(),) * 2,
            scratch_shapes=[pltpu.VMEM((ROWS, LANES), jnp.float32), pltpu.VMEM((parts, hours, LANES), jnp.float32)],
            name="pack",
        )(brightness, rate_table, control, background_std, class_index, *table)
        near = lax.all_to_all(
            payload.reshape(sources, TILES, ROWS // 2, LANES), ("gy", "gx"), 0, 0,
            axis_index_groups=[members], tiled=True
        ).reshape(rows_in_all, LANES)
        far = lax.ppermute(near, "gy", swap)
        indices, partial = pl.pallas_call(
            look_kernel(count_x, columns, hours),
            out_shape=(
                pltpu.VMEM((3, ROWS, LANES), jnp.int32),
                pltpu.VMEM((2, ROWS, LANES), jnp.float32),
            ),
            in_specs=[spec(pltpu.SMEM)] + [spec()] * 8,
            out_specs=(spec(),) * 2,
            name="look",
        )(
            brightness,
            *on_chip(near),
            *table,
            *[a.reshape(ROWS, LANES) for a in (obs_cell, obs_subhour, obs_orient, obs_value)],
        )
        whole_y = columns * cell_y + Y_SETS * ROWS * PAD
        line = count_x * ROWS * columns
        increment, departure = pl.pallas_call(
            main_kernel(count_x, columns, cell_y),
            out_shape=(array(ROWS, LANES), array(ROWS, LANES)),
            in_specs=[spec()] * 5,
            out_specs=(spec(), spec()),
            scratch_shapes=[pltpu.VMEM((2, rows_in_all + columns * PAD, LANES), jnp.float32)]
            + [pltpu.VMEM((line, LANES), jnp.float32)] * 2
            + [pltpu.VMEM((whole_y, LANES), jnp.float32)] * 3,
            name="main",
        )(*on_chip(near, far, fields, indices, partial))
        return increment, departure.reshape(obs_value.shape)

    in_specs = (
        P("gx", "gy"),
        P("gx", "gy"),
        P(None, "gx", "gy"),
        P(),
        P(None, "gx"),
        P("gx", None),
        P(),
        P(),
        P("gx", "gy", None),
        P("gx", "gy", None),
        P("gx", "gy", None),
        P("gx", "gy", None),
    )
    out_specs = (P("gx", "gy"), P("gx", "gy", None))
    return jax.shard_map(
        on_device, mesh=mesh, in_specs=in_specs, out_specs=out_specs, check_vma=False
    )
```

```python
import jax
import jax.numpy as jnp
from jax import lax
from jax.experimental import pallas as pl
from jax.experimental.pallas import tpu as pltpu
from jax.sharding import PartitionSpec as P

LANES = 128
ROWS = 8
TILES = 3
Y_SETS = 2
PAD = 8


def iota(axis):
    return lax.broadcasted_iota(jnp.int32, (ROWS, LANES), axis)


def log2(size):
    assert size & (size - 1) == 0
    return size.bit_length() - 1


def loop(count, body, carry, limit=32):
    if count <= limit:
        for at in range(count):
            carry = body(at, carry)
        return carry
    return lax.fori_loop(0, count, body, carry)


def slot(place, count):
    flip = 0
    for bit in range(1, log2(count)):
        flip = flip ^ (place >> bit & 1)
    return place ^ flip


def spread_row(row):
    return jnp.broadcast_to(row, (ROWS, LANES))


def split(wide, pieces):
    for part in range(pieces.shape[0]):
        pieces[part] = wide[:, part * LANES : (part + 1) * LANES]


def factor_tile(first_hour, parts, bright, ratios, isotropic, horizon):
    hours = ROWS // parts
    row = iota(0)
    at_hour = first_hour + (row & (hours - 1))
    near_sun, near_edge = [
        jnp.take_along_axis(bright[pl.ds(kind, ROWS, stride=0), :], at_hour, axis=1) for kind in range(2)
    ]
    sky = jnp.zeros((ROWS, LANES), jnp.float32)
    sine = sky
    sun = sky
    for part in range(parts):
        here = row >= part * hours
        sky = jnp.where(here, spread_row(isotropic[part : part + 1, :]), sky)
        sine = jnp.where(here, spread_row(horizon[part : part + 1, :]), sine)
        for hour in range(hours):
            at = first_hour + hour
            this = row == part * hours + hour
            ratio = ratios[part, pl.ds(at, 1), :]
            sun = jnp.where(this, spread_row(ratio), sun)
    return (1.0 - near_sun) * sky + near_sun * sun + near_edge * sine


def pack_kernel(count_x, columns, parts):
    def body(given, table, control, std, classes, circumsolar, isotropic, horizon, payload, fields, rates, ratios, bright):
        bright[0 : given.shape[0], 0 : given.shape[1]] = given[...]
        place_x = lax.axis_index("gx")
        place_y = lax.axis_index("gy")
        kinds, entries = table.shape
        rates[0:kinds, 0:entries] = table[...]
        rate = [
            jnp.take_along_axis(rates[pl.ds(which, ROWS, stride=0), :], classes[which], axis=1)
            for which in range(2)
        ]
        fields[0] = control[...]
        fields[1] = std[...]
        spread = control[...] * std[...] * lax.rsqrt(rate[0])
        split(circumsolar, ratios)
        mine = factor_tile(place_y * (ROWS // parts), parts, bright, ratios, isotropic, horizon)

        pairs = count_x // 2

        def put(pair, half, first, second):
            at = pl.multiple_of(pair * TILES * ROWS, ROWS)
            rows = slice(half * ROWS // 2, (half + 1) * ROWS // 2)
            payload[pl.ds(at, ROWS), :] = jnp.concatenate([spread[rows], rate[0][rows]], 0)
            payload[pl.ds(at + ROWS, ROWS), :] = jnp.concatenate([first[rows], spread[rows]], 0)
            payload[pl.ds(at + 2 * ROWS, ROWS), :] = jnp.concatenate([rate[0][rows], second[rows]], 0)

        even = slot(place_x, count_x) % 2 == 0
        first = jnp.where(even, rate[1], mine)
        second = jnp.where(even, mine, rate[1])
        for column in range(columns):

            def fill(pair, carry):
                put(column * pairs + pair, column % 2, mine, mine)
                return carry

            loop(pairs, fill, 0)
            put(column * pairs + place_x // 2, column % 2, first, second)

    return body


def look_rows(tiles, count_x, columns, keys, lane, factors):
    height = ROWS // 2

    def scan(source, factors):
        first = slot(source % count_x, count_x) * (columns * height) + source // count_x * height
        for row in range(height):
            values = tiles[pl.ds((source * TILES + 2) * height + row, ROWS, stride=0), :]
            picked = jnp.take_along_axis(values, lane, axis=1)
            factors = jnp.where(keys == first + row, picked, factors)
        return factors

    return loop(count_x * columns, scan, factors)


def look_kernel(count_x, columns, hours):
    def body(
        bright, near, circumsolar, isotropic, horizon, obs_cell, obs_subhour, obs_orient, obs_value,
        indices, partial,
    ):
        place_x = lax.axis_index("gx")
        core = lax.axis_index("gy") % 2
        hour = obs_subhour[...]
        orient = obs_orient[...]
        lane = orient & (LANES - 1)
        part_of = orient >> log2(LANES)
        home = hour - place_x * hours
        at_home = (home >= 0) & (home < hours)
        nothing = jnp.zeros((ROWS, LANES), jnp.float32)
        factors = look_rows(near, count_x, columns, jnp.where(part_of == core, hour, -1), lane, nothing)
        row = iota(0)
        for first in range(0, hours, ROWS):
            sun = nothing
            edge = nothing
            for step in range(ROWS):
                sun = jnp.where(row == step, bright[0, first + step], sun)
                edge = jnp.where(row == step, bright[1, first + step], edge)
            for part in range(2):
                ratio = circumsolar[first : first + ROWS, part * LANES : (part + 1) * LANES]
                tile = (
                    (1.0 - sun) * spread_row(isotropic[part : part + 1, :])
                    + sun * ratio
                    + edge * spread_row(horizon[part : part + 1, :])
                )
                keys = jnp.where(part_of == part, home - first, -1)
                for step in range(ROWS):
                    picked = jnp.take_along_axis(spread_row(tile[step : step + 1, :]), lane, axis=1)
                    factors = jnp.where(keys == step, picked, factors)
        indices[0] = jnp.where((part_of == core) | at_home, -1, hour)
        indices[1] = lane
        indices[2] = obs_cell[...]
        partial[0] = factors
        partial[1] = obs_value[...]

    return body


def advance(states, keep, rate, source):
    states = list(states)
    for section in range(4):
        states[section] = keep * states[section] + rate * source
        source = states[section]
    return tuple(states)


def combine(response, state):
    result = []
    for section in range(4):
        total = response[section] * state[0]
        for lower in range(1, section + 1):
            total = total + response[section - lower] * state[lower]
        result.append(total)
    return result


def main_kernel(count_x, columns, cell_y):
    assert columns % Y_SETS == 0
    steps = columns * cell_y // (Y_SETS * ROWS)
    pieces = Y_SETS * ROWS // columns
    pitch = steps + PAD
    height = ROWS // 2
    source_rows = TILES * height
    column_rows = count_x * source_rows
    column_pitch = column_rows + PAD

    def body(near, far, fields, indices, partial, increment, departure, field, ahead, smooth, source, rate, answer):
        place_x = lax.axis_index("gx")
        place_y = lax.axis_index("gy")
        core = place_y % 2
        for column in range(columns):
            taken = slice(column * column_rows, (column + 1) * column_rows)
            kept = slice(column * column_pitch, column * column_pitch + column_rows)
            field[core, kept, :] = near[taken, :]
            field[1 - core, kept, :] = far[taken, :]

        def cells(group, row, tile):
            at = slot(group, count_x) * source_rows + tile * height + row % height
            return field[row // height, pl.ds(at, columns, stride=column_pitch), :]

        def put_column(target, column, tile):
            turned = tile.T
            for part in range(pieces):
                at = (column * pieces + part) * pitch
                target[at : at + steps, 0:ROWS] = turned[part * steps : (part + 1) * steps]

        sets = range(Y_SETS)

        def strided(step, which):
            return pl.ds(which * ROWS * pitch + step, ROWS, stride=pitch)

        for row in range(ROWS):
            ahead[row * columns : (row + 1) * columns, :] = cells(place_x, row, 2)
        rates_y = [ahead[pl.ds(column, ROWS, stride=columns), :] for column in range(columns)]
        for column in range(columns):
            put_column(rate, column, rates_y[column])

        nothing = jnp.zeros((ROWS, LANES), jnp.float32)
        block = iota(0)

        def maps_of(which):
            product = nothing + 1.0
            sums = [nothing] * 3
            for step in range(steps):
                q = rate[strided(step, which), :]
                square = q * q
                product = product * (1.0 - q)
                sums = [sums[0] + q, sums[1] + square, sums[2] + square * q]
            one, two, three = sums
            return [
                product,
                product * one,
                product * ((one * one + two) * 0.5),
                product * ((one * (one * one + 3.0 * two) + 2.0 * three) * (1.0 / 6.0)),
            ]

        def shift(values, by, fill=None):
            moved = [pltpu.roll(value, by % ROWS, 0) for value in values]
            if fill is not None:
                inside = block >= by if by > 0 else block < ROWS + by
                moved = [jnp.where(inside, value, other) for value, other in zip(moved, fill)]
            return moved

        none = [nothing] * 4
        same = [nothing + 1.0] + [nothing] * 3

        def ladders(maps):
            pairs = combine(maps, shift(maps, 1))
            fours = combine(pairs, shift(pairs, 2))
            back = [maps, shift(pairs, -1), shift(fours, -3)]
            ways = []
            for way, ladder in ((1, [maps, pairs, fours]), (-1, back)):
                total = maps
                for by in (1, 2, 4):
                    total = combine(total, shift(total, way * by, same))
                ways.append((ladder, total))
            return ways

        ladders_of = [ladders(maps_of(which)) for which in sets]

        still = (jnp.zeros((columns, LANES), jnp.float32),) * 4

        def forward(group, states):
            for row in range(ROWS):
                q = cells(group, row, 1)
                states = advance(states, 1.0 - q, q, cells(group, row, 0))
                ahead[pl.ds((group * ROWS + row) * columns, columns), :] = states[3]
            return states

        def backward(turn, states):
            group = count_x - 1 - turn
            for row in range(ROWS - 1, -1, -1):
                q = cells(group, row, 1)
                at = (group * ROWS + row) * columns
                states = advance(states, 1.0 - q, q, ahead[pl.ds(at, columns), :])
                smooth[pl.ds(at, columns), :] = states[3]
            return states

        unroll = count_x if count_x <= 8 else 1
        lax.fori_loop(0, count_x, forward, still, unroll=unroll)
        lax.fori_loop(0, count_x, backward, still, unroll=unroll)

        for column in range(columns):
            tile = smooth[pl.ds(place_x * ROWS * columns + column, ROWS, stride=columns), :]
            put_column(source, column, tile * lax.rsqrt(rates_y[column]))

        def line(given, result, reverse):
            order = range(steps - 1, -1, -1) if reverse else range(steps)
            way = -1 if reverse else 1

            def run(states, store):
                states = list(states)
                for step in order:
                    for which in sets:
                        at = strided(step, which)
                        q = rate[at, :]
                        states[which] = advance(states[which], 1.0 - q, q, given[at, :])
                        if store:
                            result[at, :] = states[which][3]
                return states

            leaving = run([tuple(none)] * Y_SETS, False)
            entering = [None] * Y_SETS
            before = none
            last = 0 if reverse else ROWS - 1
            locals_of = []
            for which in sets:
                ladder, total = ladders_of[which][1 if reverse else 0]
                states = leaving[which]
                for by, maps in zip((1, 2, 4), ladder):
                    added = combine(maps, shift(states, way * by, none))
                    states = [state + more for state, more in zip(states, added)]
                locals_of.append((states, total))
            for which in reversed(sets) if reverse else sets:
                states, total = locals_of[which]
                if before is not none:
                    states = [state + more for state, more in zip(states, combine(total, before))]
                entering[which] = shift(states, way, before)
                before = [spread_row(state[last : last + 1, :]) for state in states]
            if not reverse:
                run(entering, True)
                return
            mine = place_y // (columns // Y_SETS)
            states = entering[0]
            for which in sets[1:]:
                states = [jnp.where(mine == which, new, old) for new, old in zip(entering[which], states)]
            for step in order:
                at = strided(step, mine)
                q = rate[at, :]
                states = advance(states, 1.0 - q, q, given[at, :])
                result[at, :] = states[3]

        line(source, answer, False)
        line(answer, source, True)
        own = [source[pl.ds((place_y * pieces + part) * pitch, steps), :] for part in range(pieces)]
        smooth_y = jnp.concatenate(own, 0).T[0:ROWS]
        change = fields[1] * (fields[0] + smooth_y)
        increment[...] = change

        factors = look_rows(far, count_x, columns, indices[0], indices[1], partial[0])
        cell = indices[2]
        cell_lane = cell & (LANES - 1)
        cell_row = cell >> log2(LANES)
        values = nothing
        for row in range(ROWS):
            picked = jnp.take_along_axis(spread_row(change[row : row + 1, :]), cell_lane, axis=1)
            values = jnp.where(cell_row == row, picked, values)
        departure[...] = partial[1] - factors * values

    return body


def spec(space=pltpu.VMEM):
    return pl.BlockSpec(memory_space=space)


def array(*shape):
    return jax.ShapeDtypeStruct(shape, jnp.float32)


def on_chip(*arrays):
    return [pltpu.with_memory_space_constraint(a, pltpu.VMEM) for a in arrays]


def solution(mesh):
    count_x = mesh.shape["gx"]
    columns = mesh.shape["gy"]
    sources = count_x * columns
    rows_in_all = sources * TILES * ROWS // 2
    members = [line * count_x + slot(place, count_x) for line in range(columns) for place in range(count_x)]
    swap = [(place, place ^ 1) for place in range(columns)]

    def on_device(
        control,
        background_std,
        class_index,
        rate_table,
        brightness,
        circumsolar,
        isotropic,
        horizon,
        obs_cell,
        obs_subhour,
        obs_orient,
        obs_value,
    ):
        cell_x, cell_y = control.shape
        hours, orients = circumsolar.shape
        parts = orients // LANES
        assert (cell_x, cell_y) == (ROWS, LANES) and parts == 2 and hours * parts == ROWS * columns
        assert obs_value.size == ROWS * LANES
        table = (circumsolar, isotropic.reshape(parts, LANES), horizon.reshape(parts, LANES))
        payload, fields = pl.pallas_call(
            pack_kernel(count_x, columns, parts),
            out_shape=(
                pltpu.VMEM((rows_in_all, LANES), jnp.float32),
                pltpu.VMEM((2, ROWS, LANES), jnp.float32),
            ),
            in_specs=[spec()] * 8,
            out_specs=(spec(),) * 2,
            scratch_shapes=[
                pltpu.VMEM((ROWS, LANES), jnp.float32),
                pltpu.VMEM((parts, hours, LANES), jnp.float32),
                pltpu.VMEM((ROWS, LANES), jnp.float32),
            ],
            name="pack",
        )(brightness, rate_table, control, background_std, class_index, *table)
        near = lax.all_to_all(
            payload.reshape(sources, TILES, ROWS // 2, LANES), ("gy", "gx"), 0, 0,
            axis_index_groups=[members], tiled=True
        ).reshape(rows_in_all, LANES)
        far = lax.ppermute(near, "gy", swap)
        indices, partial = pl.pallas_call(
            look_kernel(count_x, columns, hours),
            out_shape=(
                pltpu.VMEM((3, ROWS, LANES), jnp.int32),
                pltpu.VMEM((2, ROWS, LANES), jnp.float32),
            ),
            in_specs=[spec(pltpu.SMEM)] + [spec()] * 8,
            out_specs=(spec(),) * 2,
            name="look",
        )(
            brightness,
            *on_chip(near),
            *table,
            *[a.reshape(ROWS, LANES) for a in (obs_cell, obs_subhour, obs_orient, obs_value)],
        )
        whole_y = columns * cell_y + Y_SETS * ROWS * PAD
        line = count_x * ROWS * columns
        increment, departure = pl.pallas_call(
            main_kernel(count_x, columns, cell_y),
            out_shape=(array(ROWS, LANES), array(ROWS, LANES)),
            in_specs=[spec()] * 5,
            out_specs=(spec(), spec()),
            scratch_shapes=[pltpu.VMEM((2, rows_in_all + columns * PAD, LANES), jnp.float32)]
            + [pltpu.VMEM((line, LANES), jnp.float32)] * 2
            + [pltpu.VMEM((whole_y, LANES), jnp.float32)] * 3,
            name="main",
        )(*on_chip(near, far, fields, indices, partial))
        return increment, departure.reshape(obs_value.shape)

    in_specs = (
        P("gx", "gy"),
        P("gx", "gy"),
        P(None, "gx", "gy"),
        P(),
        P(None, "gx"),
        P("gx", None),
        P(),
        P(),
        P("gx", "gy", None),
        P("gx", "gy", None),
        P("gx", "gy", None),
        P("gx", "gy", None),
    )
    out_specs = (P("gx", "gy"), P("gx", "gy", None))
    return jax.shard_map(
        on_device, mesh=mesh, in_specs=in_specs, out_specs=out_specs, check_vma=False
    )
```
